32 devices in a mesh: groups: 2 (over x), seq: 16 (over z, y, core).
Axes of the slice: x: 2, y: 2, z: 4, core: 2. Of those that a mesh axis runs over, the one named last changes fastest.
Arguments:
- hidden: bfloat16 [8192, 2048], P(('groups', 'seq')), parts along dimension 0, may hold values from -6 to 6
- conv_weight: float32 [3, 2048], replicated, may hold values from -1.8 to 1.8
- feat_query_w: bfloat16 [2048, 256], replicated, may hold values from -0.125 to 0.125
- feat_key_w: bfloat16 [2048, 256], replicated, may hold values from -0.125 to 0.125
- win_query: bfloat16 [8192, 2048], P(('groups', 'seq')), parts along dimension 0, may hold values from -48 to 48
- win_key: bfloat16 [8192, 2048], P(('groups', 'seq')), parts along dimension 0, may hold values from -48 to 48
Outputs:
- mixed: bfloat16 [8192, 2048], P(('groups', 'seq')), parts along dimension 0
The draws below stay inside these ranges and needn't reach their ends.
There are 2 independent parts, one for each index of `groups`. The reference program is written for one: setup_inputs(seed, part) draws one part's arguments, and reference() takes and returns one part's arrays. A program takes and returns all parts, laid end to end along the dimension named above; an argument that names none is the same for every part. Nothing has to cross between parts.
All inputs are finite; a program needn't handle non-finite values.
Results may differ from the reference program's by a relative error of at most 0.008.
Values may be sent and summed in bfloat16 or wider, within the bound.
A program may use at most 192 MiB of HBM per device.

```python
import jax
import jax.numpy as jnp
from jax import lax

D = 2048
HEADS = 16
HEAD = 128
FEATURE_DIM = 16
WINDOW = 64
TOK_DEV = 256
SEQ_LEN = 4096
PHI = 273
N_SEQ = 16


def window_pair(key):
    first, second = jax.random.split(jax.random.fold_in(key, 7), 2)
    keys = jax.random.normal(first, (SEQ_LEN, D), jnp.float32)
    queries = jax.random.normal(second, (SEQ_LEN, D), jnp.float32)
    keys = jnp.clip(keys, -48.0, 48.0)
    queries = jnp.clip(queries, -48.0, 48.0)
    return (queries, keys)


def draw_win_query(key, part):
    return window_pair(key)[0].astype(jnp.bfloat16)


def draw_win_key(key, part):
    return window_pair(key)[1].astype(jnp.bfloat16)


def level_of(rng, extent, cuts, least, high):
    loudness = 1.0
    for axis_at, blocks in cuts:
        heights = jax.random.uniform(jax.random.fold_in(jax.random.fold_in(rng, 6), axis_at), (blocks,), jnp.float32, least / len(cuts), high / len(cuts))
        loudness = loudness * jnp.repeat(jnp.exp(heights), extent[axis_at] // blocks).reshape((-1,) + (1,) * (len(extent) - 1 - axis_at))
    return loudness


def scatter_about(stream_key, extent, spread, bound, shards=(), kind=jnp.bfloat16):
    values = jax.random.normal(stream_key, extent, jnp.float32) * spread
    if len(shards) > 0:
        values = level_of(stream_key, extent, shards, -0.22, 0.18) * values
    return jnp.clip(values, min=-bound, max=bound).astype(kind)


def setup_inputs(seed: int = 0, part: int = 0) -> dict:
    key_list = jax.random.split(jax.random.key(seed), 7)
    own_keys = jax.random.split(jax.random.fold_in(key_list[6], part), 7)
    return {
        "hidden": scatter_about(own_keys[0], (SEQ_LEN, D), 1.0, 6.0, ((0, 16),)),
        "conv_weight": scatter_about(key_list[1], (3, D), 0.6, 1.8, (), jnp.float32),
        "feat_query_w": scatter_about(key_list[2], (D, HEADS * FEATURE_DIM), D ** -0.5, 0.125),
        "feat_key_w": scatter_about(key_list[3], (D, HEADS * FEATURE_DIM), D ** -0.5, 0.125),
        "win_query": draw_win_query(jax.random.fold_in(jax.random.fold_in(key_list[6], part), 71), part),
        "win_key": draw_win_key(jax.random.fold_in(jax.random.fold_in(key_list[6], part), 71), part),
    }


def conv_rows(extended, conv_weight):
    wide = extended.astype(jnp.float32)
    total = conv_weight[0] * wide[:-2] + conv_weight[1] * wide[1:-1] + conv_weight[2] * wide[2:]
    return total.astype(jnp.bfloat16)


def taylor(features, heads):
    count = features.shape[0]
    wide = features.astype(jnp.float32).reshape(count, heads, -1)
    width = wide.shape[-1]
    first = wide * (width ** -0.25)
    second = jnp.repeat(wide, width, axis=-1) * jnp.tile(wide, (1, 1, width)) * ((width ** -0.5) / (2.0 ** 0.5))
    ones = jnp.ones((count, heads, 1), jnp.float32)
    return jnp.concatenate([ones, first, second], axis=-1).astype(jnp.bfloat16)


def mix_block(conv_blk, fq_blk, fk_blk, query, keys_ext, vals_ext, state, norm, start, heads):
    count, width = conv_blk.shape
    head = width // heads
    margin = keys_ext.shape[0] - count
    qh = query.astype(jnp.float32).reshape(count, heads, head)
    kh = keys_ext.astype(jnp.float32).reshape(count + margin, heads, head)
    vh = vals_ext.astype(jnp.float32).reshape(count + margin, heads, head)
    scores = jnp.einsum('qhd,khd->hqk', qh, kh) * (head ** -0.5)
    rows = jnp.arange(count, dtype=jnp.int32)[:, None]
    cols = jnp.arange(count + margin, dtype=jnp.int32)[None, :]
    allowed = (cols > rows) & (cols <= rows + margin) & (cols - margin + start >= 0)
    scores = jnp.where(allowed[None], scores, -jnp.inf)
    top = jnp.max(scores, axis=-1, keepdims=True)
    weights = jnp.exp(scores - top)
    probs = (weights / jnp.sum(weights, axis=-1, keepdims=True)).astype(jnp.bfloat16)
    y_win = jnp.einsum('hqk,khd->qhd', probs.astype(jnp.float32), vh)
    feature_map = fq_blk.shape[1] // heads
    feature_query_head = fq_blk.astype(jnp.float32).reshape(count, heads, feature_map)
    feature_key_head = fk_blk.astype(jnp.float32).reshape(count, heads, feature_map)
    inner_product = jnp.einsum('egz,tgz->get', feature_query_head, feature_key_head) * (feature_map ** -0.5)
    taylor_w = 1.0 + inner_product + 0.5 * inner_product * inner_product
    causal = jnp.arange(count, dtype=jnp.int32)[None, :] <= jnp.arange(count, dtype=jnp.int32)[:, None]
    taylor_w = jnp.where(causal[None], taylor_w, 0.0)
    den_in = jnp.sum(taylor_w, axis=-1)
    local_values = conv_blk.astype(jnp.float32).reshape(count, heads, head)
    num_in = jnp.einsum('hqk,khd->qhd', taylor_w.astype(jnp.bfloat16).astype(jnp.float32), local_values)
    phq = taylor(fq_blk, heads).astype(jnp.float32)
    num_out = jnp.einsum('qhf,hfd->qhd', phq, state, precision=lax.Precision.HIGHEST)
    den_out = jnp.einsum('qhf,hf->qh', phq, norm, precision=lax.Precision.HIGHEST)
    y_lin = (num_in + num_out) / (den_in.T + den_out)[..., None]
    return (y_win + y_lin).reshape(count, width).astype(jnp.bfloat16)


def block_state(conv_blk, fk_blk, heads):
    count, width = conv_blk.shape
    expanded_keys = taylor(fk_blk, heads).astype(jnp.float32)
    local_values = conv_blk.astype(jnp.float32).reshape(count, heads, width // heads)
    return jnp.einsum('jeq,jei->eqi', expanded_keys, local_values), jnp.sum(expanded_keys, axis=0)


def reference(hidden, conv_weight, feat_query_w, feat_key_w, win_query, win_key):
    width = hidden.shape[1]
    zeros_two = jnp.zeros((2, width), jnp.bfloat16)
    conv = conv_rows(jnp.concatenate([zeros_two, hidden], axis=0), conv_weight)
    fq = jnp.dot(conv, feat_query_w, preferred_element_type=jnp.float32).astype(jnp.bfloat16)
    fk = jnp.dot(conv, feat_key_w, preferred_element_type=jnp.float32).astype(jnp.bfloat16)
    pad = jnp.zeros((WINDOW, width), jnp.bfloat16)
    keys_pad = jnp.concatenate([pad, win_key], axis=0)
    vals_pad = jnp.concatenate([pad, conv], axis=0)
    init = (jnp.zeros((HEADS, PHI, HEAD), jnp.float32), jnp.zeros((HEADS, PHI), jnp.float32))

    def step(carry, block):
        state, norm = carry
        start = (block * TOK_DEV).astype(jnp.int32)
        conv_blk = lax.dynamic_slice_in_dim(conv, start, TOK_DEV, 0)
        fq_blk = lax.dynamic_slice_in_dim(fq, start, TOK_DEV, 0)
        fk_blk = lax.dynamic_slice_in_dim(fk, start, TOK_DEV, 0)
        query = lax.dynamic_slice_in_dim(win_query, start, TOK_DEV, 0)
        keys_ext = lax.dynamic_slice_in_dim(keys_pad, start, TOK_DEV + WINDOW, 0)
        vals_ext = lax.dynamic_slice_in_dim(vals_pad, start, TOK_DEV + WINDOW, 0)
        out = mix_block(conv_blk, fq_blk, fk_blk, query, keys_ext, vals_ext, state, norm, start, HEADS)
        key_value_state, ksum = block_state(conv_blk, fk_blk, HEADS)
        return (state + key_value_state, norm + ksum), out

    carry, outs = lax.scan(step, init, jnp.arange(N_SEQ, dtype=jnp.int32))
    return outs.reshape(SEQ_LEN, width)
```

```python
import functools

import jax
import jax.numpy as jnp
import numpy as np
from jax import lax
from jax.experimental import pallas as pl
from jax.experimental.pallas import tpu as pltpu
from jax.sharding import PartitionSpec as P

HEADS = 16
FEAT = 16
WINDOW = 64
CHIPS = 4
CORES = 2
TEAM = CHIPS * CORES
HALF = HEADS // CORES
OWN = HALF // CHIPS
CUTS = 2
PIECES = OWN * CUTS
ROWS = 160
QUADS = 136
GROUP = 4
LAGA = 2
LAGB = 2
TURN0 = 2
PER0 = 1
TURN1 = 8
PER1 = 1
TURNT = 3
BF = jnp.bfloat16
F32 = jnp.float32


def tables(block):
    half = FEAT // 2
    tiles = [[(i, (i + d) % half) for i in range(half)] for d in range(4)]
    tiles += [[(half + i, half + (i + d) % half) for i in range(half)] for d in range(4)]
    tiles += [[(i, half + (i + d) % half) for i in range(half)] for d in range(half)]
    tiles += [[(i, i + 4) if i < 4 else (half + i, half + i - 4) for i in range(half)]]
    sel_q = np.zeros((FEAT, 512), np.float32)
    rows_q = np.zeros((8, 256), np.float32)
    for f, (i, j) in enumerate(sum(tiles, [])):
        sel_q[i, f] = 1.0
        sel_q[j, 256 + f] = 0.5 / FEAT * (1.0 if i == j else 2.0)
    for i in range(FEAT):
        sel_q[i, QUADS + i] = 1.0
        rows_q[1, QUADS + i] = FEAT**-0.5
    rows_q[0, QUADS + FEAT] = 1.0
    rows_q[1, QUADS + FEAT] = 1.0
    return jnp.asarray(np.tile(sel_q, (block // FEAT, 1)), BF), jnp.asarray(rows_q, F32)


def nt(a, b):
    return lax.dot_general(a, b, (((1,), (1,)), ((), ())), preferred_element_type=F32)


def nn(a, b):
    return jnp.dot(a, b, preferred_element_type=F32)


def kernel(
    n, hid_h, cw_h, wq_h, wk_h, qry_h, key_h, selq_h, rowq_h, out,
    hid, cw, wq, wk, qry, key, selq, rowq,
    hprev, kprev, vprev, cv, fqs, fkt, fkf, st, rbuf, xs, rin, cin, cout, ag, bin_, obuf, sbuf, phs,
    ywin, num, den, wbias, cmask,
    loads, hs_send, hs_recv, a_send, a_recv, r_send, r_recv, c_send, c_recv, g_send, g_recv, b_send, b_recv,
):
    count, width = hid.shape
    head = width // HEADS
    me = lax.axis_index("seq")
    team = me // TEAM
    core = lax.rem(me, CORES)
    chip = lax.rem(me // CORES, CHIPS)
    teams = n // TEAM
    has_prev, has_next = me > 0, me < n - 1
    has_up, has_down = team > 0, team < teams - 1
    sibling = me + 1 - 2 * core
    mine_at, theirs_at = core * HALF, (1 - core) * HALF

    def member(other):
        return team * TEAM + other * CORES + core

    pairs = ((hid_h, hid), (cw_h, cw), (wk_h, wk), (wq_h, wq), (selq_h, selq), (rowq_h, rowq))
    fetch = [pltpu.make_async_copy(a, b, loads.at[i]) for i, (a, b) in enumerate(pairs)]

    def by_head(a, b, sem):
        for h in range(HEADS):
            pltpu.make_async_copy(a.at[:, pl.ds(h * head, head)], b.at[h], sem).start()

    fetch[0].start()
    fetch[1].start()
    by_head(key_h, key, loads.at[6])
    fetch[2].start()
    fetch[3].start()
    by_head(qry_h, qry, loads.at[7])
    fetch[4].start()
    fetch[5].start()
    fetch += [pltpu.make_async_copy(a, a, loads.at[6 + i]) for i, a in enumerate((key, qry))]

    barrier = pltpu.get_barrier_semaphore()

    def hello(dev):
        pl.semaphore_signal(barrier, inc=1, device_id={"seq": dev}, device_id_type=pl.DeviceIdType.MESH)

    hello(sibling)
    for d in range(1, CHIPS):
        hello(member(lax.rem(chip + d, CHIPS)))
    pl.when(has_prev)(lambda: hello(me - 1))
    pl.when(has_next)(lambda: hello(me + 1))
    pl.when(has_up)(lambda: hello(me - TEAM))
    pl.when(has_down)(lambda: hello(me + TEAM))
    greeted = CHIPS
    for there in (has_prev, has_next, has_up, has_down):
        greeted = greeted + there.astype(jnp.int32)
    pl.semaphore_wait(barrier, greeted)

    def remote(src, dst, send, recv, dev):
        return pltpu.make_async_remote_copy(
            src_ref=src, dst_ref=dst, send_sem=send, recv_sem=recv,
            device_id={"seq": dev}, device_id_type=pl.DeviceIdType.MESH,
        )

    tail_copy = remote(hid_h.at[pl.ds(count - 16, 16)], hprev, hs_send.at[0], hs_recv.at[0], me + 1)
    key_copy = remote(key.at[:, pl.ds(count - WINDOW, WINDOW)], kprev, hs_send.at[1], hs_recv.at[1], me + 1)
    val_copy = remote(cv.at[:, pl.ds(count - WINDOW, WINDOW)], vprev, hs_send.at[2], hs_recv.at[2], me + 1)

    pl.when(has_next)(lambda: tail_copy.start())
    fetch[6].wait()
    pl.when(has_next)(lambda: key_copy.start())

    @pl.when(jnp.logical_not(has_prev))
    def _():
        hprev[...] = jnp.zeros_like(hprev)
        kprev[...] = jnp.zeros_like(kprev)
        vprev[...] = jnp.zeros_like(vprev)

    r = lax.broadcasted_iota(jnp.int32, (count, head), 0)
    j = lax.broadcasted_iota(jnp.int32, (count, head), 1)
    rr = lax.rem(r, WINDOW)
    first = jnp.where(has_prev, 0, WINDOW)
    j = jnp.where(lax.rem(r // WINDOW, 2) == 1, lax.rem(j + WINDOW, 2 * WINDOW), j)
    ok = (j > rr) & (j <= rr + WINDOW) & ((j >= first) | (r >= WINDOW))
    wbias[...] = jnp.where(ok, 0.0, -1e30)
    half = count // 2
    r = lax.broadcasted_iota(jnp.int32, (half, half), 0)
    j = lax.broadcasted_iota(jnp.int32, (half, half), 1)
    cmask[...] = jnp.where(j <= r, 1.0, 0.0)

    for copy in fetch[:3]:
        copy.wait()
    pl.when(has_prev)(lambda: tail_copy.wait_recv())

    wide = 2 * head
    row = lax.broadcasted_iota(jnp.int32, (count, wide), 0)

    def conv_step(b, c):
        cols = pl.ds(pl.multiple_of(b * wide, wide), wide)
        h = hid[:, cols].astype(F32)
        hp = hprev[:, cols].astype(F32)
        w = cw[:, cols]
        h1 = jnp.where(row == 0, hp[15:16], pltpu.roll(h, 1, 0))
        h2 = jnp.where(row == 0, hp[14:15], jnp.where(row == 1, hp[15:16], pltpu.roll(h, 2, 0)))
        v = (w[0:1] * h2 + w[1:2] * h1 + w[2:3] * h).astype(BF)
        cv[2 * b] = v[:, :head]
        cv[2 * b + 1] = v[:, head:]
        return c

    lax.fori_loop(0, width // wide, conv_step, 0)

    def conv_rows():
        return jnp.concatenate([cv[h] for h in range(HEADS)], axis=1)

    fk = nn(conv_rows(), wk[...]).astype(BF).astype(F32)
    fk = fk.T
    fkf[...] = fk
    fkt[...] = fk.astype(BF)

    small = FEAT // 2
    srow = lax.broadcasted_iota(jnp.int32, (small, count), 0)
    unit = jnp.where(srow == 0, 1.0, 0.0)
    er = lax.broadcasted_iota(jnp.int32, (head, head), 0)
    ec = lax.broadcasted_iota(jnp.int32, (head, head), 1)
    eye = er == ec
    trow = lax.broadcasted_iota(jnp.int32, (16, head), 0)
    ones_v = jnp.ones((count, head), BF)

    def turned8(x, d):
        return pltpu.roll(x, small - d, 0) if d else x

    def key_features(h):
        k = fkf[pl.ds(pl.multiple_of(h * FEAT, FEAT), FEAT), :]
        lo, hi = k[:small], k[small:]
        rl = [turned8(lo, d) for d in range(5)]
        rh = [turned8(hi, d) for d in range(small)]
        tiles = [lo * rl[d] for d in range(4)] + [hi * rh[d] for d in range(4)]
        tiles += [lo * rh[d] for d in range(small)]
        tiles += [jnp.where(srow < 4, lo, hi) * jnp.where(srow < 4, rl[4], rh[4])]
        return jnp.concatenate(tiles + [lo, hi, unit], axis=0).astype(BF)

    def make_states(hs):
        ps = [key_features(h) for h in hs]
        vs = [cv[h] for h in hs]
        ss = [nn(p, jnp.concatenate([v, ones_v], axis=1)) for p, v in zip(ps, vs)]
        res = []
        for s in ss:
            col = s[:, head:]
            row_a = jnp.sum(jnp.where(eye, col[:head], 0.0), axis=0, keepdims=True)
            row_b = jnp.sum(jnp.where(eye[: ROWS - head], col[head:], 0.0), axis=0, keepdims=True)
            tail = jnp.where(trow == 9, row_a, jnp.where(trow == 10, row_b, s[144:, :head]))
            res.append(jnp.concatenate([s[:144, :head], tail], axis=0).astype(BF))
        for h, r in zip(hs, res):
            st[h] = r

    def to_sibling(p):
        return remote(st.at[theirs_at + p], rbuf.at[p], a_send.at[p], a_recv.at[p], sibling)

    def rows(b):
        return pl.ds(pl.multiple_of(b * (ROWS // CUTS), 16), ROWS // CUTS)

    def scatter(p, b):
        at = chip * PIECES + lax.rem(p, OWN) * CUTS + b
        return remote(
            xs.at[p, rows(b)], rin.at[chip, lax.rem(p, OWN), rows(b)], r_send.at[p * CUTS + b], r_recv.at[at], member(p // OWN)
        )

    def scattered(other, j, b):
        return remote(xs.at[0, rows(b)], rin.at[other, j, rows(b)], r_send.at[0], r_recv.at[other * PIECES + j * CUTS + b], me)

    def chain(j, b):
        q = j * CUTS + b
        return remote(cout.at[j, rows(b)], cin.at[j, rows(b)], c_send.at[q], c_recv.at[q], me + TEAM)

    def gather(other, j, b):
        q = j * CUTS + b
        return remote(
            ag.at[other, j, rows(b)], bin_.at[chip * OWN + j, rows(b)],
            g_send.at[other * PIECES + q], g_recv.at[chip * PIECES + q], member(other),
        )

    def gathered(p, b):
        return remote(ag.at[0, 0, rows(b)], bin_.at[p, rows(b)], g_send.at[0], g_recv.at[p * CUTS + b], me)

    def back(p):
        return remote(obuf.at[p], sbuf.at[mine_at + p], b_send.at[p], b_recv.at[p], sibling)

    def nth(s):
        return lax.rem(chip + 1 + lax.rem(s, CHIPS), CHIPS) * OWN + s // CHIPS

    def needed(p):
        return has_down | (chip < CHIPS - 1)

    def pass_on(p):
        to_sibling(p).wait_recv()
        both = (st[mine_at + p].astype(F32) + rbuf[p].astype(F32)).astype(BF)
        away = p // OWN != chip

        @pl.when(away & needed(p))
        def _():
            xs[p] = both
            for b in range(CUTS):
                scatter(p, b).start()

        @pl.when(jnp.logical_not(away))
        def _():
            rin[chip, lax.rem(p, OWN)] = both

    def states(s, carry):
        p = nth(s)
        make_states([theirs_at + p, mine_at + p])
        to_sibling(p).start()
        pl.when(s >= LAGA)(lambda: pass_on(nth(s - LAGA)))
        return carry

    lax.fori_loop(0, HALF, states, 0)
    for s in range(HALF - LAGA, HALF):
        pass_on(nth(s))
    pl.when(has_next)(lambda: val_copy.start())

    def own(q):
        j, b = q // CUTS, lax.rem(q, CUTS)
        part = rows(b)
        for d in range(1, CHIPS):
            other = lax.rem(chip + d, CHIPS)
            pl.when(has_down | (other < CHIPS - 1))(lambda: scattered(other, j, b).wait_recv())

        @pl.when(has_up)
        def _():
            chain(j, b).wait_recv()

        @pl.when(jnp.logical_not(has_up))
        def _():
            cin[j, part] = jnp.zeros_like(cin[j, part])

        before = cin[j, part].astype(F32)

        @pl.when(has_down)
        def _():
            total = before
            for k in range(CHIPS):
                total = total + rin[k, j, part].astype(F32)
            cout[j, part] = total.astype(BF)
            chain(j, b).start()

        for k in range(CHIPS):
            ag[k, j, part] = before.astype(BF)
            if k < CHIPS - 1:
                before = before + rin[k, j, part].astype(F32)
        for d in range(1, CHIPS):
            gather(lax.rem(chip + d, CHIPS), j, b).start()
        bin_[chip * OWN + j, part] = ag[chip, j, part]

    last = 3 * HEADS // GROUP
    turn0 = jnp.where(has_up, TURN1 + TURNT * (team - 1), TURN0)
    per = jnp.where(has_up, PER1, PER0)

    def events(i):
        def one(q, carry):
            own(q)
            return carry

        first = jnp.clip((i - turn0) * per, 0, PIECES)
        lax.fori_loop(first, jnp.clip((i + 1 - turn0) * per, 0, PIECES), one, 0)

    fetch[3].wait()
    fq = nn(conv_rows(), wq[...]).astype(BF)
    for b in range(2):
        fqs[b] = fq[:, b * 128 : (b + 1) * 128]

    lane = lax.broadcasted_iota(jnp.int32, (8, 128), 1)

    def masked_query(h):
        mask = jnp.where(lane // FEAT == lax.rem(h, 8), 1.0, 0.0)[0:1].astype(BF)
        return fqs[h // 8] * mask

    lin, sq = FEAT**-0.5, 0.5 / FEAT

    def columns(h):
        return pl.ds(pl.multiple_of(h * head, head), head)

    def linear_steps(hs):
        ms = [masked_query(h) for h in hs]
        kt = fkt[pl.ds(pl.multiple_of((hs[0] // 8) * 128, 128), 128), :]
        vbs = [jnp.concatenate([cv[h], ones_v], axis=1) for h in hs]
        x = nn(jnp.concatenate([m[:half] for m in ms], axis=0), kt[:, :half])
        a = 1.0 + x * (lin + sq * x)
        top = [(a[i * half : (i + 1) * half] * cmask[...]).astype(BF) for i in range(len(hs))]
        x = nn(jnp.concatenate([m[half:] for m in ms], axis=0), kt)
        a = 1.0 + x * (lin + sq * x)
        low = [a[i * half : (i + 1) * half] for i in range(len(hs))]
        low = [jnp.concatenate([b[:, :half], b[:, half:] * cmask[...]], axis=1).astype(BF) for b in low]
        tops = [nn(a, vb[:half]) for a, vb in zip(top, vbs)]
        lows = [nn(a, vb) for a, vb in zip(low, vbs)]
        for h, a, b in zip(hs, tops, lows):
            num[:half, columns(h)] = a[:, :head]
            den[:half, columns(h)] = a[:, head:]
            num[half:, columns(h)] = b[:, :head]
            den[half:, columns(h)] = b[:, head:]

    left = lax.broadcasted_iota(jnp.int32, (WINDOW, head), 1) < WINDOW
    ones_w = jnp.ones((2 * WINDOW, head), BF)
    scale = head**-0.5 * np.log2(np.e)

    def scores(h):
        q = qry[h]
        k = jnp.concatenate([kprev[h], key[h]], axis=0)
        w = WINDOW
        a = nt(q[: 2 * w], k[: 2 * w])
        b = nt(q[w : 3 * w], k[2 * w : 4 * w])
        c = nt(q[3 * w :], jnp.concatenate([k[4 * w :], k[3 * w : 4 * w]], axis=0))
        s = jnp.concatenate([a[:w], jnp.where(left, b[:w], a[w:]), b[w:], c], axis=0)
        return s * scale + wbias[...]

    def blend(h, p):
        w = WINDOW
        v = [vprev[h]] + [cv[h, i * w : (i + 1) * w] for i in range(count // w)]
        ys = []
        for i in range(count // w):
            pair = v[i : i + 2] if i % 2 == 0 else [v[i + 1], v[i]]
            ys.append(nn(p[i * w : (i + 1) * w], jnp.concatenate([jnp.concatenate(pair, axis=0), ones_w], axis=1)))
        return jnp.concatenate(ys, axis=0)

    def window_steps(hs):
        ss = [scores(h) for h in hs]
        ps = [jnp.exp2(s - jnp.max(s, axis=-1, keepdims=True)).astype(BF) for s in ss]
        ys = [blend(h, p) for h, p in zip(hs, ps)]
        ys = [y[:, :head] / y[:, head:] for y in ys]
        for h, y in zip(hs, ys):
            ywin[:, columns(h)] = y

    def feature_steps(hs):
        lr = nn(jnp.concatenate([masked_query(h) for h in hs], axis=0), selq[...])
        f = ((lr[:, :256] + rowq[0:1]) * (lr[:, 256:] + rowq[1:2])).astype(BF)
        for i, h in enumerate(hs):
            phs[h] = f[i * count : (i + 1) * count]

    steps = HEADS // GROUP

    def linear(i, carry):
        events(i)
        linear_steps([GROUP * i + d for d in range(GROUP)])
        return carry

    lax.fori_loop(0, steps, linear, 0)

    for copy in (fetch[4], fetch[5], fetch[7]):
        copy.wait()

    def features(i, carry):
        events(steps + i)
        feature_steps([GROUP * i + d for d in range(GROUP)])
        return carry

    lax.fori_loop(0, steps, features, 0)
    pl.when(has_prev)(lambda: key_copy.wait_recv())
    pl.when(has_prev)(lambda: val_copy.wait_recv())

    def window(i, carry):
        events(2 * steps + i)
        window_steps([GROUP * i + d for d in range(GROUP)])
        return carry

    lax.fori_loop(0, steps, window, 0)

    def late(q, carry):
        own(q)
        return carry

    lax.fori_loop(jnp.clip((last - turn0) * per, 0, PIECES), PIECES, late, 0)

    own_first = jnp.where(core == 0, 1.0, 0.0)
    spare = jnp.zeros((256 - ROWS, 2 * head), BF)

    ones_h = jnp.ones((head, head), BF)

    def final_steps(hs):
        ws = []
        for h in hs:
            s = sbuf[h]
            t = s[144:].astype(F32)
            d = jnp.concatenate(
                [jnp.where(eye, t[9:10], 0.0), jnp.where(eye[: ROWS - head], t[10:11], 0.0)], axis=0
            ).astype(BF)
            ws.append((s, d))
        ws = [(s, nn(d, ones_h).astype(BF)) for s, d in ws]
        ws = [jnp.concatenate([jnp.concatenate([s, c], axis=1), spare], axis=0) for s, c in ws]
        rs = [nn(phs[h], w) for h, w in zip(hs, ws)]
        ys = []
        for h, r in zip(hs, rs):
            cols = pl.ds(pl.multiple_of(h * head, head), head)
            ys.append((ywin[:, cols] + (num[:, cols] + r[:, :head]) / (den[:, cols] + r[:, head:])).astype(BF))
        for h, y in zip(hs, ys):
            out[:, pl.ds(pl.multiple_of(h * head, head), head)] = y

    def turned(u):
        late = u - OWN
        other = lax.rem(chip + 1 + lax.rem(late, CHIPS - 1), CHIPS)
        return jnp.where(u < OWN, chip * OWN + u, other * OWN + late // (CHIPS - 1))

    def give_back(p):
        @pl.when(p // OWN != chip)
        def _():
            for b in range(CUTS):
                gathered(p, b).wait_recv()

        before = bin_[p].astype(F32)
        at = mine_at + p
        obuf[p] = (before + own_first * st[at].astype(F32)).astype(BF)
        back(p).start()
        sbuf[at] = (before + (1.0 - own_first) * rbuf[p].astype(F32)).astype(BF)

    @pl.when(has_next)
    def _():
        tail_copy.wait_send()
        key_copy.wait_send()
        val_copy.wait_send()

    for p in range(HALF):
        to_sibling(p).wait_send()

        @pl.when((p // OWN != chip) & needed(p))
        def _(p=p):
            for b in range(CUTS):
                scatter(p, b).wait_send()


    def wind_up(u, carry):
        pl.when(u < HALF)(lambda: give_back(turned(u)))

        @pl.when(u >= LAGB)
        def _():
            p = turned(u - LAGB)
            back(p).wait_recv()
            final_steps([mine_at + p, theirs_at + p])

        return carry

    lax.fori_loop(0, HALF + LAGB, wind_up, 0)

    for p in range(HALF):
        back(p).wait_send()
    for j in range(OWN):
        for b in range(CUTS):
            pl.when(has_down)(lambda j=j, b=b: chain(j, b).wait_send())
            for d in range(1, CHIPS):
                gather(lax.rem(chip + d, CHIPS), j, b).wait_send()


def local(n, hidden, conv_weight, feat_query_w, feat_key_w, win_query, win_key):
    count, width = hidden.shape
    head = width // HEADS
    selq, rowq = tables(128)
    half = (HALF, ROWS, head)
    dma = pltpu.SemaphoreType.DMA
    return pl.pallas_call(
        functools.partial(kernel, n),
        out_shape=pltpu.VMEM((count, width), BF),
        in_specs=[pl.BlockSpec(memory_space=pl.ANY)] * 8,
        out_specs=pl.BlockSpec(memory_space=pltpu.VMEM),
        scratch_shapes=[
            pltpu.VMEM((count, width), BF),
            pltpu.VMEM(conv_weight.shape, F32),
            pltpu.VMEM(feat_query_w.shape, BF),
            pltpu.VMEM(feat_key_w.shape, BF),
            pltpu.VMEM((HEADS, count, head), BF),
            pltpu.VMEM((HEADS, count, head), BF),
            pltpu.VMEM(selq.shape, BF),
            pltpu.VMEM(rowq.shape, F32),
            pltpu.VMEM((16, width), BF),
            pltpu.VMEM((HEADS, WINDOW, head), BF),
            pltpu.VMEM((HEADS, WINDOW, head), BF),
            pltpu.VMEM((HEADS, count, head), BF),
            pltpu.VMEM((2, count, 128), BF),
            pltpu.VMEM((256, count), BF),
            pltpu.VMEM((256, count), F32),
            pltpu.VMEM((HEADS, ROWS, head), BF),
            pltpu.VMEM(half, BF),
            pltpu.VMEM(half, BF),
            pltpu.VMEM((CHIPS, OWN, ROWS, head), BF),
            pltpu.VMEM((OWN, ROWS, head), BF),
            pltpu.VMEM((OWN, ROWS, head), BF),
            pltpu.VMEM((CHIPS, OWN, ROWS, head), BF),
            pltpu.VMEM(half, BF),
            pltpu.VMEM(half, BF),
            pltpu.VMEM((HEADS, ROWS, head), BF),
            pltpu.VMEM((HEADS, count, 256), BF),
            pltpu.VMEM((count, width), F32),
            pltpu.VMEM((count, width), F32),
            pltpu.VMEM((count, width), F32),
            pltpu.VMEM((count, head), F32),
            pltpu.VMEM((count // 2, count // 2), F32),
            dma((8,)), dma((3,)), dma((3,)),
        ]
        + [dma((HALF,))] * 2 + [dma((HALF * CUTS,))] * 2 + [dma((PIECES,))] * 2 + [dma((HALF * CUTS,))] * 2 + [dma((HALF,))] * 2,
        compiler_params=pltpu.CompilerParams(
            collective_id=0, has_side_effects=True, vmem_limit_bytes=56 * 1024 * 1024
        ),
    )(hidden, conv_weight, feat_query_w, feat_key_w, win_query, win_key, selq, rowq)


def solution(mesh):
    placed = (P(("groups", "seq"), None), P(), P(), P(), P(("groups", "seq"), None), P(("groups", "seq"), None))
    return jax.shard_map(
        functools.partial(local, mesh.shape["seq"]),
        mesh=mesh, in_specs=placed, out_specs=P(("groups", "seq"), None), check_vma=False,
    )
```

```python
import functools

import jax
import jax.numpy as jnp
import numpy as np
from jax import lax
from jax.experimental import pallas as pl
from jax.experimental.pallas import tpu as pltpu
from jax.sharding import PartitionSpec as P

HEADS = 16
FEAT = 16
WINDOW = 64
CHIPS = 4
CORES = 2
TEAM = CHIPS * CORES
HALF = HEADS // CORES
OWN = HALF // CHIPS
CUTS = 2
PIECES = OWN * CUTS
ROWS = 160
QUADS = 136
GROUP = 4
LAGA = 2
LAGB = 1
PAIR = 2
TURN0 = 2
PER0 = 1
TURN1 = 8
PER1 = 1
TURNT = 3
BF = jnp.bfloat16
F32 = jnp.float32


def tables(block):
    half = FEAT // 2
    tiles = [[(i, (i + d) % half) for i in range(half)] for d in range(4)]
    tiles += [[(half + i, half + (i + d) % half) for i in range(half)] for d in range(4)]
    tiles += [[(i, half + (i + d) % half) for i in range(half)] for d in range(half)]
    tiles += [[(i, i + 4) if i < 4 else (half + i, half + i - 4) for i in range(half)]]
    sel_q = np.zeros((FEAT, 512), np.float32)
    rows_q = np.zeros((8, 256), np.float32)
    for f, (i, j) in enumerate(sum(tiles, [])):
        sel_q[i, f] = 1.0
        sel_q[j, 256 + f] = 0.5 / FEAT * (1.0 if i == j else 2.0)
    for i in range(FEAT):
        sel_q[i, QUADS + i] = 1.0
        rows_q[1, QUADS + i] = FEAT**-0.5
    rows_q[0, QUADS + FEAT] = 1.0
    rows_q[1, QUADS + FEAT] = 1.0
    return jnp.asarray(np.tile(sel_q, (block // FEAT, 1)), BF), jnp.asarray(rows_q, F32)


def nt(a, b):
    return lax.dot_general(a, b, (((1,), (1,)), ((), ())), preferred_element_type=F32)


def nn(a, b):
    return jnp.dot(a, b, preferred_element_type=F32)


def kernel(
    n, hid_h, cw_h, wq_h, wk_h, qry_h, key_h, selq_h, rowq_h, out,
    hid, cw, wq, wk, qry, key, selq, rowq,
    hprev, kprev, vprev, cv, fqs, fks, fkt, fkf, st, rbuf, xs, rin, cin, cout, ag, bin_, obuf, sbuf, phs,
    ywin, num, den, wbias, cmask,
    loads, hs_send, hs_recv, v_send, v_recv, a_send, a_recv, r_send, r_recv, c_send, c_recv, g_send, g_recv, b_send, b_recv,
):
    count, width = hid.shape
    head = width // HEADS
    me = lax.axis_index("seq")
    team = me // TEAM
    core = lax.rem(me, CORES)
    chip = lax.rem(me // CORES, CHIPS)
    teams = n // TEAM
    has_prev, has_next = me > 0, me < n - 1
    has_up, has_down = team > 0, team < teams - 1
    sibling = me + 1 - 2 * core
    mine_at, theirs_at = core * HALF, (1 - core) * HALF

    def member(other):
        return team * TEAM + other * CORES + core

    barrier = pltpu.get_barrier_semaphore()

    def hello(dev):
        pl.semaphore_signal(barrier, inc=1, device_id={"seq": dev}, device_id_type=pl.DeviceIdType.MESH)

    hello(sibling)
    for d in range(1, CHIPS):
        hello(member(lax.rem(chip + d, CHIPS)))
    pl.when(has_prev)(lambda: hello(me - 1))
    pl.when(has_next)(lambda: hello(me + 1))
    pl.when(has_up)(lambda: hello(me - TEAM))
    pl.when(has_down)(lambda: hello(me + TEAM))
    pairs = ((hid_h, hid), (cw_h, cw), (selq_h, selq), (rowq_h, rowq))
    fetch = [pltpu.make_async_copy(a, b, loads.at[i]) for i, (a, b) in enumerate(pairs)]

    def by_columns(a, b, sem):
        for h in range(a.shape[1] // head):
            pltpu.make_async_copy(a.at[:, pl.ds(h * head, head)], b.at[h], sem).start()

    fetch[0].start()
    fetch[1].start()
    by_columns(wk_h, wk, loads.at[4])
    by_columns(key_h, key, loads.at[6])
    by_columns(wq_h, wq, loads.at[5])
    by_columns(qry_h, qry, loads.at[7])
    fetch[2].start()
    fetch[3].start()
    fetch += [pltpu.make_async_copy(a, a, loads.at[4 + i]) for i, a in enumerate((wk, wq, key, qry))]

    greeted = CHIPS
    for there in (has_prev, has_next, has_up, has_down):
        greeted = greeted + there.astype(jnp.int32)
    pl.semaphore_wait(barrier, greeted)

    def remote(src, dst, send, recv, dev):
        return pltpu.make_async_remote_copy(
            src_ref=src, dst_ref=dst, send_sem=send, recv_sem=recv,
            device_id={"seq": dev}, device_id_type=pl.DeviceIdType.MESH,
        )

    tail_copy = remote(hid_h.at[pl.ds(count - 16, 16)], hprev, hs_send.at[0], hs_recv.at[0], me + 1)
    key_copy = remote(key.at[:, pl.ds(count - WINDOW, WINDOW)], kprev, hs_send.at[1], hs_recv.at[1], me + 1)

    def val_copy(g):
        part = pl.ds(g * GROUP, GROUP)
        return remote(cv.at[part, pl.ds(count - WINDOW, WINDOW)], vprev.at[part], v_send.at[g], v_recv.at[g], me + 1)


    pl.when(has_next)(lambda: tail_copy.start())
    fetch[6].wait()
    pl.when(has_next)(lambda: key_copy.start())

    @pl.when(jnp.logical_not(has_prev))
    def _():
        hprev[...] = jnp.zeros_like(hprev)
        kprev[...] = jnp.zeros_like(kprev)
        vprev[...] = jnp.zeros_like(vprev)

    r = lax.broadcasted_iota(jnp.int32, (count, head), 0)
    j = lax.broadcasted_iota(jnp.int32, (count, head), 1)
    rr = lax.rem(r, WINDOW)
    first = jnp.where(has_prev, 0, WINDOW)
    j = jnp.where(lax.rem(r // WINDOW, 2) == 1, lax.rem(j + WINDOW, 2 * WINDOW), j)
    ok = (j > rr) & (j <= rr + WINDOW) & ((j >= first) | (r >= WINDOW))
    wbias[...] = jnp.where(ok, 0.0, -1e30)
    half = count // 2
    r = lax.broadcasted_iota(jnp.int32, (half, half), 0)
    j = lax.broadcasted_iota(jnp.int32, (half, half), 1)
    cmask[...] = jnp.where(j <= r, 1.0, 0.0)

    fetch[0].wait()
    fetch[1].wait()
    wide = 2 * head
    edge = 16

    def conv_step(b, c):
        cols = pl.ds(pl.multiple_of(b * wide, wide), wide)
        h = hid[:, cols].astype(F32)
        w = cw[:, cols]
        v = (w[0:1] * pltpu.roll(h, 2, 0) + w[1:2] * pltpu.roll(h, 1, 0) + w[2:3] * h).astype(BF)
        cv[2 * b] = v[:, :head]
        cv[2 * b + 1] = v[:, head:]
        return c

    lax.fori_loop(0, width // wide, conv_step, 0)
    fetch[4].wait()
    fetch[5].wait()

    def project(rows):
        f = nn(
            jnp.concatenate([cv[h, rows] for h in range(HEADS)], axis=1),
            jnp.concatenate([wk[0], wk[1], wq[0], wq[1]], axis=1),
        ).astype(BF)
        fks[rows] = f[:, :256].astype(F32)
        for b in range(2):
            fqs[b, rows] = f[:, 256 + b * 128 : 256 + (b + 1) * 128]

    project(slice(edge, count))

    pl.when(has_prev)(lambda: tail_copy.wait_recv())
    row = lax.broadcasted_iota(jnp.int32, (edge, wide), 0)
    for b in range(width // wide):
        cols = slice(b * wide, (b + 1) * wide)
        h = hid[:edge, cols].astype(F32)
        hp = hprev[:, cols].astype(F32)
        h1 = jnp.where(row == 0, hp[15:16], pltpu.roll(h, 1, 0))
        h2 = jnp.where(row == 0, hp[14:15], jnp.where(row == 1, hp[15:16], pltpu.roll(h, 2, 0)))
        w = cw[:, cols]
        v = (w[0:1] * h2 + w[1:2] * h1 + w[2:3] * h).astype(BF)
        cv[2 * b, :edge] = v[:, :head]
        cv[2 * b + 1, :edge] = v[:, head:]
    project(slice(0, edge))
    fk = fks[...]
    fk = fk.T
    fkf[...] = fk
    fkt[...] = fk.astype(BF)

    small = FEAT // 2
    srow = lax.broadcasted_iota(jnp.int32, (small, count), 0)
    unit = jnp.where(srow == 0, 1.0, 0.0)
    er = lax.broadcasted_iota(jnp.int32, (head, head), 0)
    ec = lax.broadcasted_iota(jnp.int32, (head, head), 1)
    eye = er == ec
    trow = lax.broadcasted_iota(jnp.int32, (16, head), 0)
    ones_v = jnp.ones((count, head), BF)

    def turned8(x, d):
        return pltpu.roll(x, small - d, 0) if d else x

    def key_features(h):
        k = fkf[pl.ds(pl.multiple_of(h * FEAT, FEAT), FEAT), :]
        lo, hi = k[:small], k[small:]
        rl = [turned8(lo, d) for d in range(5)]
        rh = [turned8(hi, d) for d in range(small)]
        tiles = [lo * rl[d] for d in range(4)] + [hi * rh[d] for d in range(4)]
        tiles += [lo * rh[d] for d in range(small)]
        tiles += [jnp.where(srow < 4, lo, hi) * jnp.where(srow < 4, rl[4], rh[4])]
        return jnp.concatenate(tiles + [lo, hi, unit], axis=0).astype(BF)

    def make_states(hs):
        ps = [key_features(h) for h in hs]
        vs = [cv[h] for h in hs]
        ss = [nn(p, jnp.concatenate([v, ones_v], axis=1)) for p, v in zip(ps, vs)]
        res = []
        for s in ss:
            col = s[:, head:]
            row_a = jnp.sum(jnp.where(eye, col[:head], 0.0), axis=0, keepdims=True)
            row_b = jnp.sum(jnp.where(eye[: ROWS - head], col[head:], 0.0), axis=0, keepdims=True)
            tail = jnp.where(trow == 9, row_a, jnp.where(trow == 10, row_b, s[144:, :head]))
            res.append(jnp.concatenate([s[:144, :head], tail], axis=0).astype(BF))
        for h, r in zip(hs, res):
            st[h] = r

    def to_sibling(p):
        return remote(st.at[theirs_at + p], rbuf.at[p], a_send.at[0], a_recv.at[p], sibling)

    def rows(b):
        return pl.ds(pl.multiple_of(b * (ROWS // CUTS), 16), ROWS // CUTS)

    def scatter(p, b):
        at = chip * PIECES + lax.rem(p, OWN) * CUTS + b
        return remote(
            xs.at[p, rows(b)], rin.at[chip, lax.rem(p, OWN), rows(b)], r_send.at[0], r_recv.at[at], member(p // OWN)
        )

    def scattered(other, j, b):
        return remote(xs.at[0, rows(b)], rin.at[other, j, rows(b)], r_send.at[0], r_recv.at[other * PIECES + j * CUTS + b], me)

    def chain(j, b):
        q = j * CUTS + b
        return remote(cout.at[j, rows(b)], cin.at[j, rows(b)], c_send.at[0], c_recv.at[q], me + TEAM)

    def gather(other, j, b):
        q = j * CUTS + b
        return remote(
            ag.at[other, j, rows(b)], bin_.at[chip * OWN + j, rows(b)],
            g_send.at[0], g_recv.at[chip * PIECES + q], member(other),
        )

    def gathered(p, b):
        return remote(ag.at[0, 0, rows(b)], bin_.at[p, rows(b)], g_send.at[0], g_recv.at[p * CUTS + b], me)

    def back(p):
        return remote(obuf.at[p], sbuf.at[mine_at + p], b_send.at[0], b_recv.at[p], sibling)

    def nth(s):
        return lax.rem(chip + 1 + lax.rem(s, CHIPS), CHIPS) * OWN + s // CHIPS

    def needed(p):
        return has_down | (chip < CHIPS - 1)

    def pass_on(p):
        to_sibling(p).wait_recv()
        both = (st[mine_at + p].astype(F32) + rbuf[p].astype(F32)).astype(BF)
        away = p // OWN != chip

        @pl.when(away & needed(p))
        def _():
            xs[p] = both
            for b in range(CUTS):
                scatter(p, b).start()

        @pl.when(jnp.logical_not(away))
        def _():
            rin[chip, lax.rem(p, OWN)] = both

    def states(s, carry):
        p = nth(s)
        make_states([theirs_at + p, mine_at + p])
        to_sibling(p).start()
        pl.when(s >= LAGA)(lambda: pass_on(nth(s - LAGA)))
        return carry

    lax.fori_loop(0, HALF, states, 0)
    for s in range(HALF - LAGA, HALF):
        pass_on(nth(s))

    @pl.when(has_next)
    def _():
        for g in range(HEADS // GROUP):
            val_copy(g).start()


    def own(q):
        j, b = q // CUTS, lax.rem(q, CUTS)
        part = rows(b)
        for d in range(1, CHIPS):
            other = lax.rem(chip + d, CHIPS)
            pl.when(has_down | (other < CHIPS - 1))(lambda: scattered(other, j, b).wait_recv())

        @pl.when(has_up)
        def _():
            chain(j, b).wait_recv()

        @pl.when(jnp.logical_not(has_up))
        def _():
            cin[j, part] = jnp.zeros_like(cin[j, part])

        before = cin[j, part].astype(F32)

        @pl.when(has_down)
        def _():
            total = before
            for k in range(CHIPS):
                total = total + rin[k, j, part].astype(F32)
            cout[j, part] = total.astype(BF)
            chain(j, b).start()

        for k in range(CHIPS):
            ag[k, j, part] = before.astype(BF)
            if k < CHIPS - 1:
                before = before + rin[k, j, part].astype(F32)
        for d in range(1, CHIPS):
            gather(lax.rem(chip + d, CHIPS), j, b).start()
        bin_[chip * OWN + j, part] = ag[chip, j, part]

    last = 3 * HEADS // GROUP
    turn0 = jnp.where(has_up, TURN1 + TURNT * (team - 1), TURN0)
    per = jnp.where(has_up, PER1, PER0)

    def events(i):
        def one(q, carry):
            own(q)
            return carry

        first = jnp.clip((i - turn0) * per, 0, PIECES)
        lax.fori_loop(first, jnp.clip((i + 1 - turn0) * per, 0, PIECES), one, 0)

    lane = lax.broadcasted_iota(jnp.int32, (8, 128), 1)

    def masked_query(h):
        mask = jnp.where(lane // FEAT == lax.rem(h, 8), 1.0, 0.0)[0:1].astype(BF)
        return fqs[h // 8] * mask

    lin, sq = FEAT**-0.5, 0.5 / FEAT

    def columns(h):
        return pl.ds(pl.multiple_of(h * head, head), head)

    def linear_steps(hs):
        ms = [masked_query(h) for h in hs]
        kt = fkt[pl.ds(pl.multiple_of((hs[0] // 8) * 128, 128), 128), :]
        vbs = [jnp.concatenate([cv[h], ones_v], axis=1) for h in hs]
        x = nn(jnp.concatenate([m[:half] for m in ms], axis=0), kt[:, :half])
        a = 1.0 + x * (lin + sq * x)
        top = [(a[i * half : (i + 1) * half] * cmask[...]).astype(BF) for i in range(len(hs))]
        x = nn(jnp.concatenate([m[half:] for m in ms], axis=0), kt)
        a = 1.0 + x * (lin + sq * x)
        low = [a[i * half : (i + 1) * half] for i in range(len(hs))]
        low = [jnp.concatenate([b[:, :half], b[:, half:] * cmask[...]], axis=1).astype(BF) for b in low]
        tops = [nn(a, vb[:half]) for a, vb in zip(top, vbs)]
        lows = [nn(a, vb) for a, vb in zip(low, vbs)]
        for h, a, b in zip(hs, tops, lows):
            num[:half, columns(h)] = a[:, :head]
            den[:half, columns(h)] = a[:, head:]
            num[half:, columns(h)] = b[:, :head]
            den[half:, columns(h)] = b[:, head:]

    left = lax.broadcasted_iota(jnp.int32, (WINDOW, head), 1) < WINDOW
    ones_w = jnp.ones((2 * WINDOW, head), BF)
    scale = head**-0.5 * np.log2(np.e)

    def scores(h):
        q = qry[h]
        k = jnp.concatenate([kprev[h], key[h]], axis=0)
        w = WINDOW
        a = nt(q[: 2 * w], k[: 2 * w])
        b = nt(q[w : 3 * w], k[2 * w : 4 * w])
        c = nt(q[3 * w :], jnp.concatenate([k[4 * w :], k[3 * w : 4 * w]], axis=0))
        s = jnp.concatenate([a[:w], jnp.where(left, b[:w], a[w:]), b[w:], c], axis=0)
        return s * scale + wbias[...]

    def blend(h, p):
        w = WINDOW
        v = [vprev[h]] + [cv[h, i * w : (i + 1) * w] for i in range(count // w)]
        ys = []
        for i in range(count // w):
            pair = v[i : i + 2] if i % 2 == 0 else [v[i + 1], v[i]]
            ys.append(nn(p[i * w : (i + 1) * w], jnp.concatenate([jnp.concatenate(pair, axis=0), ones_w], axis=1)))
        return jnp.concatenate(ys, axis=0)

    def window_steps(hs):
        ss = [scores(h) for h in hs]
        ps = [jnp.exp2(s - jnp.max(s, axis=-1, keepdims=True)).astype(BF) for s in ss]
        ys = [blend(h, p) for h, p in zip(hs, ps)]
        ys = [y[:, :head] / y[:, head:] for y in ys]
        for h, y in zip(hs, ys):
            ywin[:, columns(h)] = y

    def feature_steps(hs):
        lr = nn(jnp.concatenate([masked_query(h) for h in hs], axis=0), selq[...])
        f = ((lr[:, :256] + rowq[0:1]) * (lr[:, 256:] + rowq[1:2])).astype(BF)
        for i, h in enumerate(hs):
            phs[h] = f[i * count : (i + 1) * count]

    steps = HEADS // GROUP

    def linear(i, carry):
        events(i)
        linear_steps([GROUP * i + d for d in range(GROUP)])
        return carry

    lax.fori_loop(0, steps, linear, 0)

    for copy in (fetch[2], fetch[3], fetch[7]):
        copy.wait()

    def features(i, carry):
        events(steps + i)
        feature_steps([GROUP * i + d for d in range(GROUP)])
        return carry

    lax.fori_loop(0, steps, features, 0)
    pl.when(has_prev)(lambda: key_copy.wait_recv())

    def window(i, carry):
        events(2 * steps + i)
        pl.when(has_prev)(lambda: val_copy(i).wait_recv())
        window_steps([GROUP * i + d for d in range(GROUP)])
        return carry

    lax.fori_loop(0, steps, window, 0)

    def late(q, carry):
        own(q)
        return carry

    lax.fori_loop(jnp.clip((last - turn0) * per, 0, PIECES), PIECES, late, 0)

    own_first = jnp.where(core == 0, 1.0, 0.0)
    spare = jnp.zeros((256 - ROWS, 2 * head), BF)

    ones_h = jnp.ones((head, head), BF)

    def final_steps(hs):
        ws = []
        for h in hs:
            s = sbuf[h]
            t = s[144:].astype(F32)
            d = jnp.concatenate(
                [jnp.where(eye, t[9:10], 0.0), jnp.where(eye[: ROWS - head], t[10:11], 0.0)], axis=0
            ).astype(BF)
            ws.append((s, d))
        ws = [(s, nn(d, ones_h).astype(BF)) for s, d in ws]
        ws = [jnp.concatenate([jnp.concatenate([s, c], axis=1), spare], axis=0) for s, c in ws]
        rs = [nn(phs[h], w) for h, w in zip(hs, ws)]
        ys = []
        for h, r in zip(hs, rs):
            cols = pl.ds(pl.multiple_of(h * head, head), head)
            ys.append((ywin[:, cols] + (num[:, cols] + r[:, :head]) / (den[:, cols] + r[:, head:])).astype(BF))
        for h, y in zip(hs, ys):
            out[:, pl.ds(pl.multiple_of(h * head, head), head)] = y

    def turned(u):
        late = u - OWN
        other = lax.rem(chip + 1 + lax.rem(late, CHIPS - 1), CHIPS)
        return jnp.where(u < OWN, chip * OWN + u, other * OWN + late // (CHIPS - 1))

    def give_back(p):
        @pl.when(p // OWN != chip)
        def _():
            for b in range(CUTS):
                gathered(p, b).wait_recv()

        before = bin_[p].astype(F32)
        at = mine_at + p
        obuf[p] = (before + own_first * st[at].astype(F32)).astype(BF)
        back(p).start()
        sbuf[at] = (before + (1.0 - own_first) * rbuf[p].astype(F32)).astype(BF)

    @pl.when(has_next)
    def _():
        tail_copy.wait_send()
        key_copy.wait_send()
        for g in range(HEADS // GROUP):
            val_copy(g).wait_send()

    remote(st.at[pl.ds(0, HALF)], st.at[pl.ds(0, HALF)], a_send.at[0], a_recv.at[0], sibling).wait_send()

    @pl.when(has_down | (chip < CHIPS - 1))
    def _():
        away = pl.ds(0, HALF - OWN)
        remote(xs.at[away], xs.at[away], r_send.at[0], r_recv.at[0], sibling).wait_send()

    def wind_up(u, carry):
        @pl.when(u < HALF // PAIR)
        def _():
            for i in range(PAIR):
                give_back(turned(PAIR * u + i))

        @pl.when(u >= LAGB)
        def _():
            ps = [turned(PAIR * (u - LAGB) + i) for i in range(PAIR)]
            for p in ps:
                back(p).wait_recv()
            final_steps([at + p for p in ps for at in (mine_at, theirs_at)])

        return carry

    lax.fori_loop(0, HALF // PAIR + LAGB, wind_up, 0)

    remote(obuf, obuf, b_send.at[0], b_recv.at[0], sibling).wait_send()
    away = pl.ds(0, CHIPS - 1)
    remote(ag.at[away], ag.at[away], g_send.at[0], g_recv.at[0], sibling).wait_send()
    pl.when(has_down)(lambda: remote(cout, cout, c_send.at[0], c_recv.at[0], sibling).wait_send())


def local(n, hidden, conv_weight, feat_query_w, feat_key_w, win_query, win_key):
    count, width = hidden.shape
    head = width // HEADS
    selq, rowq = tables(128)
    half = (HALF, ROWS, head)
    dma = pltpu.SemaphoreType.DMA
    return pl.pallas_call(
        functools.partial(kernel, n),
        out_shape=pltpu.VMEM((count, width), BF),
        in_specs=[pl.BlockSpec(memory_space=pl.ANY)] * 8,
        out_specs=pl.BlockSpec(memory_space=pltpu.VMEM),
        scratch_shapes=[
            pltpu.VMEM((count, width), BF),
            pltpu.VMEM(conv_weight.shape, F32),
            pltpu.VMEM((2, width, head), BF),
            pltpu.VMEM((2, width, head), BF),
            pltpu.VMEM((HEADS, count, head), BF),
            pltpu.VMEM((HEADS, count, head), BF),
            pltpu.VMEM(selq.shape, BF),
            pltpu.VMEM(rowq.shape, F32),
            pltpu.VMEM((16, width), BF),
            pltpu.VMEM((HEADS, WINDOW, head), BF),
            pltpu.VMEM((HEADS, WINDOW, head), BF),
            pltpu.VMEM((HEADS, count, head), BF),
            pltpu.VMEM((2, count, 128), BF),
            pltpu.VMEM((count, 256), F32),
            pltpu.VMEM((256, count), BF),
            pltpu.VMEM((256, count), F32),
            pltpu.VMEM((HEADS, ROWS, head), BF),
            pltpu.VMEM(half, BF),
            pltpu.VMEM(half, BF),
            pltpu.VMEM((CHIPS, OWN, ROWS, head), BF),
            pltpu.VMEM((OWN, ROWS, head), BF),
            pltpu.VMEM((OWN, ROWS, head), BF),
            pltpu.VMEM((CHIPS, OWN, ROWS, head), BF),
            pltpu.VMEM(half, BF),
            pltpu.VMEM(half, BF),
            pltpu.VMEM((HEADS, ROWS, head), BF),
            pltpu.VMEM((HEADS, count, 256), BF),
            pltpu.VMEM((count, width), F32),
            pltpu.VMEM((count, width), F32),
            pltpu.VMEM((count, width), F32),
            pltpu.VMEM((count, head), F32),
            pltpu.VMEM((count // 2, count // 2), F32),
            dma((8,)), dma((2,)), dma((2,)),
            dma((HEADS // GROUP,)), dma((HEADS // GROUP,)),
        ]
        + [
            dma((1,)), dma((HALF,)), dma((1,)), dma((HALF * CUTS,)), dma((1,)), dma((PIECES,)),
            dma((1,)), dma((HALF * CUTS,)), dma((1,)), dma((HALF,)),
        ],
        compiler_params=pltpu.CompilerParams(
            collective_id=0, has_side_effects=True, vmem_limit_bytes=56 * 1024 * 1024
        ),
    )(hidden, conv_weight, feat_query_w, feat_key_w, win_query, win_key, selq, rowq)


def solution(mesh):
    placed = (P(("groups", "seq"), None), P(), P(), P(), P(("groups", "seq"), None), P(("groups", "seq"), None))
    return jax.shard_map(
        functools.partial(local, mesh.shape["seq"]),
        mesh=mesh, in_specs=placed, out_specs=P(("groups", "seq"), None), check_vma=False,
    )
```

```python
import functools

import jax
import jax.numpy as jnp
import numpy as np
from jax import lax
from jax.experimental import pallas as pl
from jax.experimental.pallas import tpu as pltpu
from jax.sharding import PartitionSpec as P

HEADS = 16
FEAT = 16
WINDOW = 64
CHIPS = 4
CORES = 2
TEAM = CHIPS * CORES
HALF = HEADS // CORES
OWN = HALF // CHIPS
CUTS = 2
PIECES = OWN * CUTS
ROWS = 160
QUADS = 136
GROUP = 4
TURNV = 0
LAGB = 1
PAIR = 2
TURN0 = 2
PER0 = 1
TURN1 = 5
PER1 = 1
TURNT = 3
BF = jnp.bfloat16
F32 = jnp.float32


def tables(block):
    half = FEAT // 2
    tiles = [[(i, (i + d) % half) for i in range(half)] for d in range(4)]
    tiles += [[(half + i, half + (i + d) % half) for i in range(half)] for d in range(4)]
    tiles += [[(i, half + (i + d) % half) for i in range(half)] for d in range(half)]
    tiles += [[(i, i + 4) if i < 4 else (half + i, half + i - 4) for i in range(half)]]
    sel_q = np.zeros((FEAT, 512), np.float32)
    rows_q = np.zeros((8, 256), np.float32)
    for f, (i, j) in enumerate(sum(tiles, [])):
        sel_q[i, f] = 1.0
        sel_q[j, 256 + f] = 0.5 / FEAT * (1.0 if i == j else 2.0)
    for i in range(FEAT):
        sel_q[i, QUADS + i] = 1.0
        rows_q[1, QUADS + i] = FEAT**-0.5
    rows_q[0, QUADS + FEAT] = 1.0
    rows_q[1, QUADS + FEAT] = 1.0
    return jnp.asarray(np.tile(sel_q, (block // FEAT, 1)), BF), jnp.asarray(rows_q, F32)


def nt(a, b):
    return lax.dot_general(a, b, (((1,), (1,)), ((), ())), preferred_element_type=F32)


def nn(a, b):
    return jnp.dot(a, b, preferred_element_type=F32)


def kernel(
    n, hid_h, cw_h, wq_h, wk_h, qry_h, key_h, selq_h, rowq_h, out,
    hid, cw, wq, wk, qry, key, selq, rowq,
    hprev, kprev, vprev, cv, fqs, fks, fkt, fkf, st, rbuf, xs, rin, cin, cout, ag, bin_, obuf, sbuf, phs,
    ywin, num, den, wbias, cmask,
    loads, hs_send, hs_recv, v_send, v_recv, a_send, a_recv, r_send, r_recv, c_send, c_recv, g_send, g_recv, b_send, b_recv,
):
    count, width = hid.shape
    head = width // HEADS
    me = lax.axis_index("seq")
    team = me // TEAM
    core = lax.rem(me, CORES)
    chip = lax.rem(me // CORES, CHIPS)
    teams = n // TEAM
    has_prev, has_next = me > 0, me < n - 1
    has_up, has_down = team > 0, team < teams - 1
    sibling = me + 1 - 2 * core
    mine_at, theirs_at = core * HALF, (1 - core) * HALF

    def member(other):
        return team * TEAM + other * CORES + core

    barrier = pltpu.get_barrier_semaphore()

    def hello(dev):
        pl.semaphore_signal(barrier, inc=1, device_id={"seq": dev}, device_id_type=pl.DeviceIdType.MESH)

    hello(sibling)
    for d in range(1, CHIPS):
        hello(member(lax.rem(chip + d, CHIPS)))
    pl.when(has_prev)(lambda: hello(me - 1))
    pl.when(has_next)(lambda: hello(me + 1))
    pl.when(has_up)(lambda: hello(me - TEAM))
    pl.when(has_down)(lambda: hello(me + TEAM))
    pairs = ((hid_h, hid), (cw_h, cw), (selq_h, selq), (rowq_h, rowq))
    fetch = [pltpu.make_async_copy(a, b, loads.at[i]) for i, (a, b) in enumerate(pairs)]

    def by_columns(a, b, sem):
        for h in range(a.shape[1] // head):
            pltpu.make_async_copy(a.at[:, pl.ds(h * head, head)], b.at[h], sem).start()

    fetch[0].start()
    fetch[1].start()
    by_columns(wk_h, wk, loads.at[4])
    by_columns(key_h, key, loads.at[6])
    by_columns(wq_h, wq, loads.at[5])
    by_columns(qry_h, qry, loads.at[7])
    fetch[2].start()
    fetch[3].start()
    fetch += [pltpu.make_async_copy(a, a, loads.at[4 + i]) for i, a in enumerate((wk, wq, key, qry))]

    greeted = CHIPS
    for there in (has_prev, has_next, has_up, has_down):
        greeted = greeted + there.astype(jnp.int32)
    pl.semaphore_wait(barrier, greeted)

    def remote(src, dst, send, recv, dev):
        return pltpu.make_async_remote_copy(
            src_ref=src, dst_ref=dst, send_sem=send, recv_sem=recv,
            device_id={"seq": dev}, device_id_type=pl.DeviceIdType.MESH,
        )

    tail_copy = remote(hid_h.at[pl.ds(count - 16, 16)], hprev, hs_send.at[0], hs_recv.at[0], me + 1)
    key_copy = remote(key.at[:, pl.ds(count - WINDOW, WINDOW)], kprev, hs_send.at[1], hs_recv.at[1], me + 1)

    def val_copy(g):
        part = pl.ds(g * GROUP, GROUP)
        return remote(cv.at[part, pl.ds(count - WINDOW, WINDOW)], vprev.at[part], v_send.at[g], v_recv.at[g], me + 1)


    pl.when(has_next)(lambda: tail_copy.start())
    fetch[6].wait()
    pl.when(has_next)(lambda: key_copy.start())

    @pl.when(jnp.logical_not(has_prev))
    def _():
        hprev[...] = jnp.zeros_like(hprev)
        kprev[...] = jnp.zeros_like(kprev)
        vprev[...] = jnp.zeros_like(vprev)

    r = lax.broadcasted_iota(jnp.int32, (count, head), 0)
    j = lax.broadcasted_iota(jnp.int32, (count, head), 1)
    rr = lax.rem(r, WINDOW)
    first = jnp.where(has_prev, 0, WINDOW)
    j = jnp.where(lax.rem(r // WINDOW, 2) == 1, lax.rem(j + WINDOW, 2 * WINDOW), j)
    ok = (j > rr) & (j <= rr + WINDOW) & ((j >= first) | (r >= WINDOW))
    wbias[...] = jnp.where(ok, 0.0, -1e30)
    half = count // 2
    r = lax.broadcasted_iota(jnp.int32, (half, half), 0)
    j = lax.broadcasted_iota(jnp.int32, (half, half), 1)
    cmask[...] = jnp.where(j <= r, 1.0, 0.0)

    fetch[0].wait()
    fetch[1].wait()
    wide = 2 * head
    edge = 16

    def conv_step(b, c):
        cols = pl.ds(pl.multiple_of(b * wide, wide), wide)
        h = hid[:, cols].astype(F32)
        w = cw[:, cols]
        v = (w[0:1] * pltpu.roll(h, 2, 0) + w[1:2] * pltpu.roll(h, 1, 0) + w[2:3] * h).astype(BF)
        cv[2 * b] = v[:, :head]
        cv[2 * b + 1] = v[:, head:]
        return c

    lax.fori_loop(0, width // wide, conv_step, 0)
    fetch[4].wait()
    fetch[5].wait()

    def project(rows):
        f = nn(
            jnp.concatenate([cv[h, rows] for h in range(HEADS)], axis=1),
            jnp.concatenate([wk[0], wk[1], wq[0], wq[1]], axis=1),
        ).astype(BF)
        fks[rows] = f[:, :256].astype(F32)
        for b in range(2):
            fqs[b, rows] = f[:, 256 + b * 128 : 256 + (b + 1) * 128]

    project(slice(edge, count))

    pl.when(has_prev)(lambda: tail_copy.wait_recv())
    row = lax.broadcasted_iota(jnp.int32, (edge, wide), 0)
    for b in range(width // wide):
        cols = slice(b * wide, (b + 1) * wide)
        h = hid[:edge, cols].astype(F32)
        hp = hprev[:, cols].astype(F32)
        h1 = jnp.where(row == 0, hp[15:16], pltpu.roll(h, 1, 0))
        h2 = jnp.where(row == 0, hp[14:15], jnp.where(row == 1, hp[15:16], pltpu.roll(h, 2, 0)))
        w = cw[:, cols]
        v = (w[0:1] * h2 + w[1:2] * h1 + w[2:3] * h).astype(BF)
        cv[2 * b, :edge] = v[:, :head]
        cv[2 * b + 1, :edge] = v[:, head:]
    project(slice(0, edge))
    fk = fks[...]
    fk = fk.T
    fkf[...] = fk
    fkt[...] = fk.astype(BF)

    small = FEAT // 2
    srow = lax.broadcasted_iota(jnp.int32, (small, count), 0)
    unit = jnp.where(srow == 0, 1.0, 0.0)
    er = lax.broadcasted_iota(jnp.int32, (head, head), 0)
    ec = lax.broadcasted_iota(jnp.int32, (head, head), 1)
    eye = er == ec
    trow = lax.broadcasted_iota(jnp.int32, (16, head), 0)
    ones_v = jnp.ones((count, head), BF)

    def turned8(x, d):
        return pltpu.roll(x, small - d, 0) if d else x

    def key_features(h):
        k = fkf[pl.ds(pl.multiple_of(h * FEAT, FEAT), FEAT), :]
        lo, hi = k[:small], k[small:]
        rl = [turned8(lo, d) for d in range(5)]
        rh = [turned8(hi, d) for d in range(small)]
        tiles = [lo * rl[d] for d in range(4)] + [hi * rh[d] for d in range(4)]
        tiles += [lo * rh[d] for d in range(small)]
        tiles += [jnp.where(srow < 4, lo, hi) * jnp.where(srow < 4, rl[4], rh[4])]
        return jnp.concatenate(tiles + [lo, hi, unit], axis=0).astype(BF)

    def make_states(hs):
        ps = [key_features(h) for h in hs]
        vs = [cv[h] for h in hs]
        ss = [nn(p, jnp.concatenate([v, ones_v], axis=1)) for p, v in zip(ps, vs)]
        res = []
        for s in ss:
            col = s[:, head:]
            row_a = jnp.sum(jnp.where(eye, col[:head], 0.0), axis=0, keepdims=True)
            row_b = jnp.sum(jnp.where(eye[: ROWS - head], col[head:], 0.0), axis=0, keepdims=True)
            tail = jnp.where(trow == 9, row_a, jnp.where(trow == 10, row_b, s[144:, :head]))
            res.append(jnp.concatenate([s[:144, :head], tail], axis=0).astype(BF))
        for h, r in zip(hs, res):
            st[h] = r

    def to_sibling(p):
        return remote(st.at[theirs_at + p], rbuf.at[p], a_send.at[0], a_recv.at[p], sibling)

    def rows(b):
        return pl.ds(pl.multiple_of(b * (ROWS // CUTS), 16), ROWS // CUTS)

    def scatter(p, b):
        at = chip * PIECES + lax.rem(p, OWN) * CUTS + b
        return remote(
            xs.at[p, rows(b)], rin.at[chip, lax.rem(p, OWN), rows(b)], r_send.at[0], r_recv.at[at], member(p // OWN)
        )

    def scattered(other, j, b):
        return remote(xs.at[0, rows(b)], rin.at[other, j, rows(b)], r_send.at[0], r_recv.at[other * PIECES + j * CUTS + b], me)

    def chain(j, b):
        q = j * CUTS + b
        return remote(cout.at[j, rows(b)], cin.at[j, rows(b)], c_send.at[0], c_recv.at[q], me + TEAM)

    def gather(other, j, b):
        q = j * CUTS + b
        return remote(
            ag.at[other, j, rows(b)], bin_.at[chip * OWN + j, rows(b)],
            g_send.at[0], g_recv.at[chip * PIECES + q], member(other),
        )

    def gathered(p, b):
        return remote(ag.at[0, 0, rows(b)], bin_.at[p, rows(b)], g_send.at[0], g_recv.at[p * CUTS + b], me)

    def back(p):
        return remote(obuf.at[p], sbuf.at[mine_at + p], b_send.at[0], b_recv.at[p], sibling)

    def nth(s):
        return lax.rem(chip + 1 + lax.rem(s, CHIPS), CHIPS) * OWN + s // CHIPS

    def needed(p):
        return has_down | (chip < CHIPS - 1)

    def pass_on(p):
        to_sibling(p).wait_recv()
        both = (st[mine_at + p].astype(F32) + rbuf[p].astype(F32)).astype(BF)
        away = p // OWN != chip

        @pl.when(away & needed(p))
        def _():
            xs[p] = both
            for b in range(CUTS):
                scatter(p, b).start()

        @pl.when(jnp.logical_not(away))
        def _():
            rin[chip, lax.rem(p, OWN)] = both

    def pair(t):
        return [nth(2 * t), nth(2 * t + 1)]

    def send(ps):
        for p in ps:
            to_sibling(p).start()

    def states(t, carry):
        now, later = pair(t), pair(t + 1)
        make_states([theirs_at + p for p in later] + [mine_at + p for p in now])
        send(later)
        for p in now:
            pass_on(p)
        return carry

    make_states([theirs_at + p for p in pair(0)])
    send(pair(0))
    lax.fori_loop(0, HALF // 2 - 1, states, 0)
    make_states([mine_at + p for p in pair(HALF // 2 - 1)])
    for p in pair(HALF // 2 - 1):
        pass_on(p)

    def send_values(i):
        @pl.when(has_next & (i == TURNV))
        def _():
            for g in range(HEADS // GROUP):
                val_copy(g).start()

    def own(q):
        j, b = q // CUTS, lax.rem(q, CUTS)
        part = rows(b)
        for d in range(1, CHIPS):
            other = lax.rem(chip + d, CHIPS)
            pl.when(has_down | (other < CHIPS - 1))(lambda: scattered(other, j, b).wait_recv())

        @pl.when(has_up)
        def _():
            chain(j, b).wait_recv()

        @pl.when(jnp.logical_not(has_up))
        def _():
            cin[j, part] = jnp.zeros_like(cin[j, part])

        before = cin[j, part].astype(F32)

        @pl.when(has_down)
        def _():
            total = before
            for k in range(CHIPS):
                total = total + rin[k, j, part].astype(F32)
            cout[j, part] = total.astype(BF)
            chain(j, b).start()

        for k in range(CHIPS):
            ag[k, j, part] = before.astype(BF)
            if k < CHIPS - 1:
                before = before + rin[k, j, part].astype(F32)
        for d in range(1, CHIPS):
            gather(lax.rem(chip + d, CHIPS), j, b).start()
        bin_[chip * OWN + j, part] = ag[chip, j, part]

    last = 2 * HEADS // GROUP
    turn0 = jnp.where(has_up, TURN1 + TURNT * (team - 1), TURN0)
    per = jnp.where(has_up, PER1, PER0)

    def events(i):
        def one(q, carry):
            own(q)
            return carry

        first = jnp.clip((i - turn0) * per, 0, PIECES)
        lax.fori_loop(first, jnp.clip((i + 1 - turn0) * per, 0, PIECES), one, 0)

    lane = lax.broadcasted_iota(jnp.int32, (8, 128), 1)

    def masked_query(h):
        mask = jnp.where(lane // FEAT == lax.rem(h, 8), 1.0, 0.0)[0:1].astype(BF)
        return fqs[h // 8] * mask

    lin, sq = FEAT**-0.5, 0.5 / FEAT

    def columns(h):
        return pl.ds(pl.multiple_of(h * head, head), head)

    def linear_steps(hs):
        ms = [masked_query(h) for h in hs]
        kt = fkt[pl.ds(pl.multiple_of((hs[0] // 8) * 128, 128), 128), :]
        vbs = [jnp.concatenate([cv[h], ones_v], axis=1) for h in hs]
        x = nn(jnp.concatenate([m[:half] for m in ms], axis=0), kt[:, :half])
        a = 1.0 + x * (lin + sq * x)
        top = [(a[i * half : (i + 1) * half] * cmask[...]).astype(BF) for i in range(len(hs))]
        x = nn(jnp.concatenate([m[half:] for m in ms], axis=0), kt)
        a = 1.0 + x * (lin + sq * x)
        low = [a[i * half : (i + 1) * half] for i in range(len(hs))]
        low = [jnp.concatenate([b[:, :half], b[:, half:] * cmask[...]], axis=1).astype(BF) for b in low]
        tops = [nn(a, vb[:half]) for a, vb in zip(top, vbs)]
        lows = [nn(a, vb) for a, vb in zip(low, vbs)]
        for h, a, b in zip(hs, tops, lows):
            num[:half, columns(h)] = a[:, :head]
            den[:half, columns(h)] = a[:, head:]
            num[half:, columns(h)] = b[:, :head]
            den[half:, columns(h)] = b[:, head:]

    left = lax.broadcasted_iota(jnp.int32, (WINDOW, head), 1) < WINDOW
    ones_w = jnp.ones((2 * WINDOW, head), BF)
    scale = head**-0.5 * np.log2(np.e)

    def scores(h):
        q = qry[h]
        k = jnp.concatenate([kprev[h], key[h]], axis=0)
        w = WINDOW
        a = nt(q[: 2 * w], k[: 2 * w])
        b = nt(q[w : 3 * w], k[2 * w : 4 * w])
        c = nt(q[3 * w :], jnp.concatenate([k[4 * w :], k[3 * w : 4 * w]], axis=0))
        s = jnp.concatenate([a[:w], jnp.where(left, b[:w], a[w:]), b[w:], c], axis=0)
        return s * scale + wbias[...]

    def blend(h, p):
        w = WINDOW
        v = [vprev[h]] + [cv[h, i * w : (i + 1) * w] for i in range(count // w)]
        ys = []
        for i in range(count // w):
            pair = v[i : i + 2] if i % 2 == 0 else [v[i + 1], v[i]]
            ys.append(nn(p[i * w : (i + 1) * w], jnp.concatenate([jnp.concatenate(pair, axis=0), ones_w], axis=1)))
        return jnp.concatenate(ys, axis=0)

    def window_steps(hs):
        ss = [scores(h) for h in hs]
        ps = [jnp.exp2(s - jnp.max(s, axis=-1, keepdims=True)).astype(BF) for s in ss]
        ys = [blend(h, p) for h, p in zip(hs, ps)]
        ys = [y[:, :head] / y[:, head:] for y in ys]
        for h, y in zip(hs, ys):
            ywin[:, columns(h)] = y

    def feature_steps(hs):
        lr = nn(jnp.concatenate([masked_query(h) for h in hs], axis=0), selq[...])
        f = ((lr[:, :256] + rowq[0:1]) * (lr[:, 256:] + rowq[1:2])).astype(BF)
        for i, h in enumerate(hs):
            phs[h] = f[i * count : (i + 1) * count]

    steps = HEADS // GROUP

    for copy in (fetch[2], fetch[3], fetch[7]):
        copy.wait()

    def linear(i, carry):
        send_values(i)
        events(i)
        hs = [GROUP * i + d for d in range(GROUP)]
        feature_steps(hs)
        linear_steps(hs)
        return carry

    lax.fori_loop(0, steps, linear, 0)

    pl.when(has_prev)(lambda: key_copy.wait_recv())

    def window(i, carry):
        events(steps + i)
        pl.when(has_prev)(lambda: val_copy(i).wait_recv())
        window_steps([GROUP * i + d for d in range(GROUP)])
        return carry

    lax.fori_loop(0, steps, window, 0)

    def late(q, carry):
        own(q)
        return carry

    lax.fori_loop(jnp.clip((last - turn0) * per, 0, PIECES), PIECES, late, 0)

    own_first = jnp.where(core == 0, 1.0, 0.0)
    spare = jnp.zeros((256 - ROWS, 2 * head), BF)

    ones_h = jnp.ones((head, head), BF)

    def final_steps(hs):
        ws = []
        for h in hs:
            s = sbuf[h]
            t = s[144:].astype(F32)
            d = jnp.concatenate(
                [jnp.where(eye, t[9:10], 0.0), jnp.where(eye[: ROWS - head], t[10:11], 0.0)], axis=0
            ).astype(BF)
            ws.append((s, d))
        ws = [(s, nn(d, ones_h).astype(BF)) for s, d in ws]
        ws = [jnp.concatenate([jnp.concatenate([s, c], axis=1), spare], axis=0) for s, c in ws]
        rs = [nn(phs[h], w) for h, w in zip(hs, ws)]
        ys = []
        for h, r in zip(hs, rs):
            cols = pl.ds(pl.multiple_of(h * head, head), head)
            ys.append((ywin[:, cols] + (num[:, cols] + r[:, :head]) / (den[:, cols] + r[:, head:])).astype(BF))
        for h, y in zip(hs, ys):
            out[:, pl.ds(pl.multiple_of(h * head, head), head)] = y

    def turned(u):
        late = u - OWN
        other = lax.rem(chip + 1 + lax.rem(late, CHIPS - 1), CHIPS)
        return jnp.where(u < OWN, chip * OWN + u, other * OWN + late // (CHIPS - 1))

    def give_back(p):
        @pl.when(p // OWN != chip)
        def _():
            for b in range(CUTS):
                gathered(p, b).wait_recv()

        before = bin_[p].astype(F32)
        at = mine_at + p
        obuf[p] = (before + own_first * st[at].astype(F32)).astype(BF)
        back(p).start()
        sbuf[at] = (before + (1.0 - own_first) * rbuf[p].astype(F32)).astype(BF)

    @pl.when(has_next)
    def _():
        tail_copy.wait_send()
        key_copy.wait_send()
        for g in range(HEADS // GROUP):
            val_copy(g).wait_send()

    remote(st.at[pl.ds(0, HALF)], st.at[pl.ds(0, HALF)], a_send.at[0], a_recv.at[0], sibling).wait_send()

    @pl.when(has_down | (chip < CHIPS - 1))
    def _():
        away = pl.ds(0, HALF - OWN)
        remote(xs.at[away], xs.at[away], r_send.at[0], r_recv.at[0], sibling).wait_send()

    def wind_up(u, carry):
        @pl.when(u < HALF // PAIR)
        def _():
            for i in range(PAIR):
                give_back(turned(PAIR * u + i))

        @pl.when(u >= LAGB)
        def _():
            ps = [turned(PAIR * (u - LAGB) + i) for i in range(PAIR)]
            for p in ps:
                back(p).wait_recv()
            final_steps([at + p for p in ps for at in (mine_at, theirs_at)])

        return carry

    lax.fori_loop(0, HALF // PAIR + LAGB, wind_up, 0)

    remote(obuf, obuf, b_send.at[0], b_recv.at[0], sibling).wait_send()
    away = pl.ds(0, CHIPS - 1)
    remote(ag.at[away], ag.at[away], g_send.at[0], g_recv.at[0], sibling).wait_send()
    pl.when(has_down)(lambda: remote(cout, cout, c_send.at[0], c_recv.at[0], sibling).wait_send())


def local(n, hidden, conv_weight, feat_query_w, feat_key_w, win_query, win_key):
    count, width = hidden.shape
    head = width // HEADS
    selq, rowq = tables(128)
    half = (HALF, ROWS, head)
    dma = pltpu.SemaphoreType.DMA
    return pl.pallas_call(
        functools.partial(kernel, n),
        out_shape=pltpu.VMEM((count, width), BF),
        in_specs=[pl.BlockSpec(memory_space=pl.ANY)] * 8,
        out_specs=pl.BlockSpec(memory_space=pltpu.VMEM),
        scratch_shapes=[
            pltpu.VMEM((count, width), BF),
            pltpu.VMEM(conv_weight.shape, F32),
            pltpu.VMEM((2, width, head), BF),
            pltpu.VMEM((2, width, head), BF),
            pltpu.VMEM((HEADS, count, head), BF),
            pltpu.VMEM((HEADS, count, head), BF),
            pltpu.VMEM(selq.shape, BF),
            pltpu.VMEM(rowq.shape, F32),
            pltpu.VMEM((16, width), BF),
            pltpu.VMEM((HEADS, WINDOW, head), BF),
            pltpu.VMEM((HEADS, WINDOW, head), BF),
            pltpu.VMEM((HEADS, count, head), BF),
            pltpu.VMEM((2, count, 128), BF),
            pltpu.VMEM((count, 256), F32),
            pltpu.VMEM((256, count), BF),
            pltpu.VMEM((256, count), F32),
            pltpu.VMEM((HEADS, ROWS, head), BF),
            pltpu.VMEM(half, BF),
            pltpu.VMEM(half, BF),
            pltpu.VMEM((CHIPS, OWN, ROWS, head), BF),
            pltpu.VMEM((OWN, ROWS, head), BF),
            pltpu.VMEM((OWN, ROWS, head), BF),
            pltpu.VMEM((CHIPS, OWN, ROWS, head), BF),
            pltpu.VMEM(half, BF),
            pltpu.VMEM(half, BF),
            pltpu.VMEM((HEADS, ROWS, head), BF),
            pltpu.VMEM((HEADS, count, 256), BF),
            pltpu.VMEM((count, width), F32),
            pltpu.VMEM((count, width), F32),
            pltpu.VMEM((count, width), F32),
            pltpu.VMEM((count, head), F32),
            pltpu.VMEM((count // 2, count // 2), F32),
            dma((8,)), dma((2,)), dma((2,)),
            dma((HEADS // GROUP,)), dma((HEADS // GROUP,)),
        ]
        + [
            dma((1,)), dma((HALF,)), dma((1,)), dma((HALF * CUTS,)), dma((1,)), dma((PIECES,)),
            dma((1,)), dma((HALF * CUTS,)), dma((1,)), dma((HALF,)),
        ],
        compiler_params=pltpu.CompilerParams(
            collective_id=0, has_side_effects=True, vmem_limit_bytes=56 * 1024 * 1024
        ),
    )(hidden, conv_weight, feat_query_w, feat_key_w, win_query, win_key, selq, rowq)


def solution(mesh):
    placed = (P(("groups", "seq"), None), P(), P(), P(), P(("groups", "seq"), None), P(("groups", "seq"), None))
    return jax.shard_map(
        functools.partial(local, mesh.shape["seq"]),
        mesh=mesh, in_specs=placed, out_specs=P(("groups", "seq"), None), check_vma=False,
    )
```

```python
import functools

import jax
import jax.numpy as jnp
import numpy as np
from jax import lax
from jax.experimental import pallas as pl
from jax.experimental.pallas import tpu as pltpu
from jax.sharding import PartitionSpec as P

HEADS = 16
FEAT = 16
WINDOW = 64
CHIPS = 4
CORES = 2
TEAM = CHIPS * CORES
HALF = HEADS // CORES
OWN = HALF // CHIPS
CUTS = 1
PIECES = OWN * CUTS
ROWS = 160
QUADS = 136
GROUP = 4
TURNV = 0
LAGB = 1
PAIR = 2
TURN0 = 2
PER0 = 1
TURN1 = 6
PER1 = 1
TURNT = 3
BF = jnp.bfloat16
F32 = jnp.float32


def tables(block):
    half = FEAT // 2
    tiles = [[(i, (i + d) % half) for i in range(half)] for d in range(4)]
    tiles += [[(half + i, half + (i + d) % half) for i in range(half)] for d in range(4)]
    tiles += [[(i, half + (i + d) % half) for i in range(half)] for d in range(half)]
    tiles += [[(i, i + 4) if i < 4 else (half + i, half + i - 4) for i in range(half)]]
    sel_q = np.zeros((FEAT, 512), np.float32)
    rows_q = np.zeros((8, 256), np.float32)
    for f, (i, j) in enumerate(sum(tiles, [])):
        sel_q[i, f] = 1.0
        sel_q[j, 256 + f] = 0.5 / FEAT * (1.0 if i == j else 2.0)
    for i in range(FEAT):
        sel_q[i, QUADS + i] = 1.0
        rows_q[1, QUADS + i] = FEAT**-0.5
    rows_q[0, QUADS + FEAT] = 1.0
    rows_q[1, QUADS + FEAT] = 1.0
    return jnp.asarray(np.tile(sel_q, (block // FEAT, 1)), BF), jnp.asarray(rows_q, F32)


def nt(a, b):
    return lax.dot_general(a, b, (((1,), (1,)), ((), ())), preferred_element_type=F32)


def nn(a, b):
    return jnp.dot(a, b, preferred_element_type=F32)


def kernel(
    n, hid_h, cw_h, wq_h, wk_h, qry_h, key_h, selq_h, rowq_h, out,
    hid, cw, wq, wk, qry, key, selq, rowq,
    hprev, kprev, vprev, cv, fqs, fks, fkt, fkf, st, rbuf, xs, rin, cin, cout, ag, bin_, obuf, sbuf, phs,
    ywin, num, den, wbias, cmask,
    loads, hs_send, hs_recv, v_send, v_recv, a_send, a_recv, r_send, r_recv, c_send, c_recv, g_send, g_recv, b_send, b_recv,
):
    count, width = hid.shape
    head = width // HEADS
    me = lax.axis_index("seq")
    team = me // TEAM
    core = lax.rem(me, CORES)
    chip = lax.rem(me // CORES, CHIPS)
    teams = n // TEAM
    has_prev, has_next = me > 0, me < n - 1
    has_up, has_down = team > 0, team < teams - 1
    sibling = me + 1 - 2 * core
    mine_at, theirs_at = core * HALF, (1 - core) * HALF

    def member(other):
        return team * TEAM + other * CORES + core

    barrier = pltpu.get_barrier_semaphore()

    def hello(dev):
        pl.semaphore_signal(barrier, inc=1, device_id={"seq": dev}, device_id_type=pl.DeviceIdType.MESH)

    hello(sibling)
    for d in range(1, CHIPS):
        hello(member(lax.rem(chip + d, CHIPS)))
    pl.when(has_prev)(lambda: hello(me - 1))
    pl.when(has_next)(lambda: hello(me + 1))
    pl.when(has_up)(lambda: hello(me - TEAM))
    pl.when(has_down)(lambda: hello(me + TEAM))
    pairs = ((hid_h, hid), (cw_h, cw), (selq_h, selq), (rowq_h, rowq))
    fetch = [pltpu.make_async_copy(a, b, loads.at[i]) for i, (a, b) in enumerate(pairs)]

    def by_columns(a, b, sem):
        for h in range(a.shape[1] // head):
            pltpu.make_async_copy(a.at[:, pl.ds(h * head, head)], b.at[h], sem).start()

    fetch[0].start()
    fetch[1].start()
    by_columns(wk_h, wk, loads.at[4])
    by_columns(key_h, key, loads.at[6])
    by_columns(wq_h, wq, loads.at[5])
    by_columns(qry_h, qry, loads.at[7])
    fetch[2].start()
    fetch[3].start()
    fetch += [pltpu.make_async_copy(a, a, loads.at[4 + i]) for i, a in enumerate((wk, wq, key, qry))]

    greeted = CHIPS
    for there in (has_prev, has_next, has_up, has_down):
        greeted = greeted + there.astype(jnp.int32)
    pl.semaphore_wait(barrier, greeted)

    def remote(src, dst, send, recv, dev):
        return pltpu.make_async_remote_copy(
            src_ref=src, dst_ref=dst, send_sem=send, recv_sem=recv,
            device_id={"seq": dev}, device_id_type=pl.DeviceIdType.MESH,
        )

    tail_copy = remote(hid_h.at[pl.ds(count - 16, 16)], hprev, hs_send.at[0], hs_recv.at[0], me + 1)
    key_copy = remote(key.at[:, pl.ds(count - WINDOW, WINDOW)], kprev, hs_send.at[1], hs_recv.at[1], me + 1)

    def val_copy(g):
        part = pl.ds(g * GROUP, GROUP)
        return remote(cv.at[part, pl.ds(count - WINDOW, WINDOW)], vprev.at[part], v_send.at[g], v_recv.at[g], me + 1)


    pl.when(has_next)(lambda: tail_copy.start())
    fetch[6].wait()
    pl.when(has_next)(lambda: key_copy.start())

    @pl.when(jnp.logical_not(has_prev))
    def _():
        hprev[...] = jnp.zeros_like(hprev)
        kprev[...] = jnp.zeros_like(kprev)
        vprev[...] = jnp.zeros_like(vprev)

    r = lax.broadcasted_iota(jnp.int32, (count, head), 0)
    j = lax.broadcasted_iota(jnp.int32, (count, head), 1)
    rr = lax.rem(r, WINDOW)
    first = jnp.where(has_prev, 0, WINDOW)
    j = jnp.where(lax.rem(r // WINDOW, 2) == 1, lax.rem(j + WINDOW, 2 * WINDOW), j)
    ok = (j > rr) & (j <= rr + WINDOW) & ((j >= first) | (r >= WINDOW))
    wbias[...] = jnp.where(ok, 0.0, -1e30)
    half = count // 2
    r = lax.broadcasted_iota(jnp.int32, (half, half), 0)
    j = lax.broadcasted_iota(jnp.int32, (half, half), 1)
    cmask[...] = jnp.where(j <= r, 1.0, 0.0)

    fetch[0].wait()
    fetch[1].wait()
    wide = 2 * head
    edge = 16

    def conv_step(b, c):
        cols = pl.ds(pl.multiple_of(b * wide, wide), wide)
        h = hid[:, cols].astype(F32)
        w = cw[:, cols]
        v = (w[0:1] * pltpu.roll(h, 2, 0) + w[1:2] * pltpu.roll(h, 1, 0) + w[2:3] * h).astype(BF)
        cv[2 * b] = v[:, :head]
        cv[2 * b + 1] = v[:, head:]
        return c

    lax.fori_loop(0, width // wide, conv_step, 0)
    fetch[4].wait()
    fetch[5].wait()

    def project(rows):
        f = nn(
            jnp.concatenate([cv[h, rows] for h in range(HEADS)], axis=1),
            jnp.concatenate([wk[0], wk[1], wq[0], wq[1]], axis=1),
        ).astype(BF)
        fks[rows] = f[:, :256].astype(F32)
        for b in range(2):
            fqs[b, rows] = f[:, 256 + b * 128 : 256 + (b + 1) * 128]

    project(slice(edge, count))

    pl.when(has_prev)(lambda: tail_copy.wait_recv())
    row = lax.broadcasted_iota(jnp.int32, (edge, wide), 0)
    for b in range(width // wide):
        cols = slice(b * wide, (b + 1) * wide)
        h = hid[:edge, cols].astype(F32)
        hp = hprev[:, cols].astype(F32)
        h1 = jnp.where(row == 0, hp[15:16], pltpu.roll(h, 1, 0))
        h2 = jnp.where(row == 0, hp[14:15], jnp.where(row == 1, hp[15:16], pltpu.roll(h, 2, 0)))
        w = cw[:, cols]
        v = (w[0:1] * h2 + w[1:2] * h1 + w[2:3] * h).astype(BF)
        cv[2 * b, :edge] = v[:, :head]
        cv[2 * b + 1, :edge] = v[:, head:]
    project(slice(0, edge))
    fk = fks[...]
    fk = fk.T
    fkf[...] = fk
    fkt[...] = fk.astype(BF)

    small = FEAT // 2
    srow = lax.broadcasted_iota(jnp.int32, (small, count), 0)
    unit = jnp.where(srow == 0, 1.0, 0.0)
    er = lax.broadcasted_iota(jnp.int32, (head, head), 0)
    ec = lax.broadcasted_iota(jnp.int32, (head, head), 1)
    eye = er == ec
    trow = lax.broadcasted_iota(jnp.int32, (16, head), 0)
    ones_v = jnp.ones((count, head), BF)

    def turned8(x, d):
        return pltpu.roll(x, small - d, 0) if d else x

    def key_features(h):
        k = fkf[pl.ds(pl.multiple_of(h * FEAT, FEAT), FEAT), :]
        lo, hi = k[:small], k[small:]
        rl = [turned8(lo, d) for d in range(5)]
        rh = [turned8(hi, d) for d in range(small)]
        tiles = [lo * rl[d] for d in range(4)] + [hi * rh[d] for d in range(4)]
        tiles += [lo * rh[d] for d in range(small)]
        tiles += [jnp.where(srow < 4, lo, hi) * jnp.where(srow < 4, rl[4], rh[4])]
        return jnp.concatenate(tiles + [lo, hi, unit], axis=0).astype(BF)

    def make_states(hs):
        ps = [key_features(h) for h in hs]
        vs = [cv[h] for h in hs]
        ss = [nn(p, jnp.concatenate([v, ones_v], axis=1)) for p, v in zip(ps, vs)]
        res = []
        for s in ss:
            col = s[:, head:]
            row_a = jnp.sum(jnp.where(eye, col[:head], 0.0), axis=0, keepdims=True)
            row_b = jnp.sum(jnp.where(eye[: ROWS - head], col[head:], 0.0), axis=0, keepdims=True)
            tail = jnp.where(trow == 9, row_a, jnp.where(trow == 10, row_b, s[144:, :head]))
            res.append(jnp.concatenate([s[:144, :head], tail], axis=0).astype(BF))
        for h, r in zip(hs, res):
            st[h] = r

    def to_sibling(p):
        return remote(st.at[theirs_at + p], rbuf.at[p], a_send.at[0], a_recv.at[p], sibling)

    def rows(b):
        return pl.ds(pl.multiple_of(b * (ROWS // CUTS), 16), ROWS // CUTS)

    def scatter(p, b):
        at = chip * PIECES + lax.rem(p, OWN) * CUTS + b
        return remote(
            xs.at[p, rows(b)], rin.at[chip, lax.rem(p, OWN), rows(b)], r_send.at[0], r_recv.at[at], member(p // OWN)
        )

    def scattered(other, j, b):
        return remote(xs.at[0, rows(b)], rin.at[other, j, rows(b)], r_send.at[0], r_recv.at[other * PIECES + j * CUTS + b], me)

    def chain(j, b):
        q = j * CUTS + b
        return remote(cout.at[j, rows(b)], cin.at[j, rows(b)], c_send.at[0], c_recv.at[q], me + TEAM)

    def gather(other, j, b):
        q = j * CUTS + b
        return remote(
            ag.at[other, j, rows(b)], bin_.at[chip * OWN + j, rows(b)],
            g_send.at[0], g_recv.at[chip * PIECES + q], member(other),
        )

    def gathered(p, b):
        return remote(ag.at[0, 0, rows(b)], bin_.at[p, rows(b)], g_send.at[0], g_recv.at[p * CUTS + b], me)

    def back(p):
        return remote(obuf.at[p], sbuf.at[mine_at + p], b_send.at[0], b_recv.at[p], sibling)

    def nth(s):
        return lax.rem(chip + 1 + lax.rem(s, CHIPS), CHIPS) * OWN + s // CHIPS

    def needed(p):
        return has_down | (chip < CHIPS - 1)

    def pass_on(p):
        to_sibling(p).wait_recv()
        both = (st[mine_at + p].astype(F32) + rbuf[p].astype(F32)).astype(BF)
        away = p // OWN != chip

        @pl.when(away & needed(p))
        def _():
            xs[p] = both
            for b in range(CUTS):
                scatter(p, b).start()

        @pl.when(jnp.logical_not(away))
        def _():
            rin[chip, lax.rem(p, OWN)] = both

    def pair(t):
        return [nth(2 * t), nth(2 * t + 1)]

    def send(ps):
        for p in ps:
            to_sibling(p).start()

    def states(t, carry):
        now, later = pair(t), pair(t + 1)
        make_states([theirs_at + p for p in later] + [mine_at + p for p in now])
        send(later)
        for p in now:
            pass_on(p)
        return carry

    make_states([theirs_at + p for p in pair(0)])
    send(pair(0))
    lax.fori_loop(0, HALF // 2 - 1, states, 0)
    make_states([mine_at + p for p in pair(HALF // 2 - 1)])
    for p in pair(HALF // 2 - 1):
        pass_on(p)

    def send_values(i):
        @pl.when(has_next & (i == TURNV))
        def _():
            for g in range(HEADS // GROUP):
                val_copy(g).start()

    def own(q):
        j, b = q // CUTS, lax.rem(q, CUTS)
        part = rows(b)
        for d in range(1, CHIPS):
            other = lax.rem(chip + d, CHIPS)
            pl.when(has_down | (other < CHIPS - 1))(lambda: scattered(other, j, b).wait_recv())

        @pl.when(has_up)
        def _():
            chain(j, b).wait_recv()

        @pl.when(jnp.logical_not(has_up))
        def _():
            cin[j, part] = jnp.zeros_like(cin[j, part])

        before = cin[j, part].astype(F32)

        @pl.when(has_down)
        def _():
            total = before
            for k in range(CHIPS):
                total = total + rin[k, j, part].astype(F32)
            cout[j, part] = total.astype(BF)
            chain(j, b).start()

        for k in range(CHIPS):
            ag[k, j, part] = before.astype(BF)
            pl.when(chip != k)(lambda k=k: gather(k, j, b).start())
            if k < CHIPS - 1:
                before = before + rin[k, j, part].astype(F32)
        bin_[chip * OWN + j, part] = ag[chip, j, part]

    last = 2 * HEADS // GROUP
    turn0 = jnp.where(has_up, TURN1 + TURNT * (team - 1), TURN0)
    per = jnp.where(has_up, PER1, PER0)

    def events(i):
        def one(q, carry):
            own(q)
            return carry

        first = jnp.clip((i - turn0) * per, 0, PIECES)
        lax.fori_loop(first, jnp.clip((i + 1 - turn0) * per, 0, PIECES), one, 0)

    lane = lax.broadcasted_iota(jnp.int32, (8, 128), 1)

    def masked_query(h):
        mask = jnp.where(lane // FEAT == lax.rem(h, 8), 1.0, 0.0)[0:1].astype(BF)
        return fqs[h // 8] * mask

    lin, sq = FEAT**-0.5, 0.5 / FEAT

    def columns(h):
        return pl.ds(pl.multiple_of(h * head, head), head)

    def linear_steps(hs):
        ms = [masked_query(h) for h in hs]
        kt = fkt[pl.ds(pl.multiple_of((hs[0] // 8) * 128, 128), 128), :]
        vbs = [jnp.concatenate([cv[h], ones_v], axis=1) for h in hs]
        x = nn(jnp.concatenate([m[:half] for m in ms], axis=0), kt[:, :half])
        a = 1.0 + x * (lin + sq * x)
        top = [(a[i * half : (i + 1) * half] * cmask[...]).astype(BF) for i in range(len(hs))]
        x = nn(jnp.concatenate([m[half:] for m in ms], axis=0), kt)
        a = 1.0 + x * (lin + sq * x)
        low = [a[i * half : (i + 1) * half] for i in range(len(hs))]
        low = [jnp.concatenate([b[:, :half], b[:, half:] * cmask[...]], axis=1).astype(BF) for b in low]
        tops = [nn(a, vb[:half]) for a, vb in zip(top, vbs)]
        lows = [nn(a, vb) for a, vb in zip(low, vbs)]
        for h, a, b in zip(hs, tops, lows):
            num[:half, columns(h)] = a[:, :head]
            den[:half, columns(h)] = a[:, head:]
            num[half:, columns(h)] = b[:, :head]
            den[half:, columns(h)] = b[:, head:]

    left = lax.broadcasted_iota(jnp.int32, (WINDOW, head), 1) < WINDOW
    ones_w = jnp.ones((2 * WINDOW, head), BF)
    scale = head**-0.5 * np.log2(np.e)

    def scores(h):
        q = qry[h]
        k = jnp.concatenate([kprev[h], key[h]], axis=0)
        w = WINDOW
        a = nt(q[: 2 * w], k[: 2 * w])
        b = nt(q[w : 3 * w], k[2 * w : 4 * w])
        c = nt(q[3 * w :], jnp.concatenate([k[4 * w :], k[3 * w : 4 * w]], axis=0))
        s = jnp.concatenate([a[:w], jnp.where(left, b[:w], a[w:]), b[w:], c], axis=0)
        return s * scale + wbias[...]

    def blend(h, p):
        w = WINDOW
        v = [vprev[h]] + [cv[h, i * w : (i + 1) * w] for i in range(count // w)]
        ys = []
        for i in range(count // w):
            pair = v[i : i + 2] if i % 2 == 0 else [v[i + 1], v[i]]
            ys.append(nn(p[i * w : (i + 1) * w], jnp.concatenate([jnp.concatenate(pair, axis=0), ones_w], axis=1)))
        return jnp.concatenate(ys, axis=0)

    def window_steps(hs):
        ss = [scores(h) for h in hs]
        ps = [jnp.exp2(s - jnp.max(s, axis=-1, keepdims=True)).astype(BF) for s in ss]
        ys = [blend(h, p) for h, p in zip(hs, ps)]
        ys = [y[:, :head] / y[:, head:] for y in ys]
        for h, y in zip(hs, ys):
            ywin[:, columns(h)] = y

    def feature_steps(hs):
        lr = nn(jnp.concatenate([masked_query(h) for h in hs], axis=0), selq[...])
        f = ((lr[:, :256] + rowq[0:1]) * (lr[:, 256:] + rowq[1:2])).astype(BF)
        for i, h in enumerate(hs):
            phs[h] = f[i * count : (i + 1) * count]

    steps = HEADS // GROUP

    for copy in (fetch[2], fetch[3], fetch[7]):
        copy.wait()

    def linear(i, carry):
        send_values(i)
        events(i)
        hs = [GROUP * i + d for d in range(GROUP)]
        feature_steps(hs)
        linear_steps(hs)
        return carry

    lax.fori_loop(0, steps, linear, 0)

    pl.when(has_prev)(lambda: key_copy.wait_recv())

    def window(i, carry):
        events(steps + i)
        pl.when(has_prev)(lambda: val_copy(i).wait_recv())
        window_steps([GROUP * i + d for d in range(GROUP)])
        return carry

    lax.fori_loop(0, steps, window, 0)

    def late(q, carry):
        own(q)
        return carry

    lax.fori_loop(jnp.clip((last - turn0) * per, 0, PIECES), PIECES, late, 0)

    own_first = jnp.where(core == 0, 1.0, 0.0)
    spare = jnp.zeros((256 - ROWS, 2 * head), BF)

    ones_h = jnp.ones((head, head), BF)

    def final_steps(hs):
        ws = []
        for h in hs:
            s = sbuf[h]
            t = s[144:].astype(F32)
            d = jnp.concatenate(
                [jnp.where(eye, t[9:10], 0.0), jnp.where(eye[: ROWS - head], t[10:11], 0.0)], axis=0
            ).astype(BF)
            ws.append((s, d))
        ws = [(s, nn(d, ones_h).astype(BF)) for s, d in ws]
        ws = [jnp.concatenate([jnp.concatenate([s, c], axis=1), spare], axis=0) for s, c in ws]
        rs = [nn(phs[h], w) for h, w in zip(hs, ws)]
        ys = []
        for h, r in zip(hs, rs):
            cols = pl.ds(pl.multiple_of(h * head, head), head)
            ys.append((ywin[:, cols] + (num[:, cols] + r[:, :head]) / (den[:, cols] + r[:, head:])).astype(BF))
        for h, y in zip(hs, ys):
            out[:, pl.ds(pl.multiple_of(h * head, head), head)] = y

    def turned(u):
        late = u - OWN
        other = lax.rem(chip + 1 + lax.rem(late, CHIPS - 1), CHIPS)
        return jnp.where(u < OWN, chip * OWN + u, other * OWN + late // (CHIPS - 1))

    def give_back(p):
        @pl.when(p // OWN != chip)
        def _():
            for b in range(CUTS):
                gathered(p, b).wait_recv()

        before = bin_[p].astype(F32)
        at = mine_at + p
        obuf[p] = (before + own_first * st[at].astype(F32)).astype(BF)
        back(p).start()
        sbuf[at] = (before + (1.0 - own_first) * rbuf[p].astype(F32)).astype(BF)

    @pl.when(has_next)
    def _():
        tail_copy.wait_send()
        key_copy.wait_send()
        for g in range(HEADS // GROUP):
            val_copy(g).wait_send()

    remote(st.at[pl.ds(0, HALF)], st.at[pl.ds(0, HALF)], a_send.at[0], a_recv.at[0], sibling).wait_send()

    @pl.when(has_down | (chip < CHIPS - 1))
    def _():
        away = pl.ds(0, HALF - OWN)
        remote(xs.at[away], xs.at[away], r_send.at[0], r_recv.at[0], sibling).wait_send()

    def wind_up(u, carry):
        @pl.when(u < HALF // PAIR)
        def _():
            for i in range(PAIR):
                give_back(turned(PAIR * u + i))

        @pl.when(u >= LAGB)
        def _():
            ps = [turned(PAIR * (u - LAGB) + i) for i in range(PAIR)]
            for p in ps:
                back(p).wait_recv()
            final_steps([at + p for p in ps for at in (mine_at, theirs_at)])

        return carry

    lax.fori_loop(0, HALF // PAIR + LAGB, wind_up, 0)

    remote(obuf, obuf, b_send.at[0], b_recv.at[0], sibling).wait_send()
    away = pl.ds(0, CHIPS - 1)
    remote(ag.at[away], ag.at[away], g_send.at[0], g_recv.at[0], sibling).wait_send()
    pl.when(has_down)(lambda: remote(cout, cout, c_send.at[0], c_recv.at[0], sibling).wait_send())


def local(n, hidden, conv_weight, feat_query_w, feat_key_w, win_query, win_key):
    count, width = hidden.shape
    head = width // HEADS
    selq, rowq = tables(128)
    half = (HALF, ROWS, head)
    dma = pltpu.SemaphoreType.DMA
    return pl.pallas_call(
        functools.partial(kernel, n),
        out_shape=pltpu.VMEM((count, width), BF),
        in_specs=[pl.BlockSpec(memory_space=pl.ANY)] * 8,
        out_specs=pl.BlockSpec(memory_space=pltpu.VMEM),
        scratch_shapes=[
            pltpu.VMEM((count, width), BF),
            pltpu.VMEM(conv_weight.shape, F32),
            pltpu.VMEM((2, width, head), BF),
            pltpu.VMEM((2, width, head), BF),
            pltpu.VMEM((HEADS, count, head), BF),
            pltpu.VMEM((HEADS, count, head), BF),
            pltpu.VMEM(selq.shape, BF),
            pltpu.VMEM(rowq.shape, F32),
            pltpu.VMEM((16, width), BF),
            pltpu.VMEM((HEADS, WINDOW, head), BF),
            pltpu.VMEM((HEADS, WINDOW, head), BF),
            pltpu.VMEM((HEADS, count, head), BF),
            pltpu.VMEM((2, count, 128), BF),
            pltpu.VMEM((count, 256), F32),
            pltpu.VMEM((256, count), BF),
            pltpu.VMEM((256, count), F32),
            pltpu.VMEM((HEADS, ROWS, head), BF),
            pltpu.VMEM(half, BF),
            pltpu.VMEM(half, BF),
            pltpu.VMEM((CHIPS, OWN, ROWS, head), BF),
            pltpu.VMEM((OWN, ROWS, head), BF),
            pltpu.VMEM((OWN, ROWS, head), BF),
            pltpu.VMEM((CHIPS, OWN, ROWS, head), BF),
            pltpu.VMEM(half, BF),
            pltpu.VMEM(half, BF),
            pltpu.VMEM((HEADS, ROWS, head), BF),
            pltpu.VMEM((HEADS, count, 256), BF),
            pltpu.VMEM((count, width), F32),
            pltpu.VMEM((count, width), F32),
            pltpu.VMEM((count, width), F32),
            pltpu.VMEM((count, head), F32),
            pltpu.VMEM((count // 2, count // 2), F32),
            dma((8,)), dma((2,)), dma((2,)),
            dma((HEADS // GROUP,)), dma((HEADS // GROUP,)),
        ]
        + [
            dma((1,)), dma((HALF,)), dma((1,)), dma((HALF * CUTS,)), dma((1,)), dma((PIECES,)),
            dma((1,)), dma((HALF * CUTS,)), dma((1,)), dma((HALF,)),
        ],
        compiler_params=pltpu.CompilerParams(
            collective_id=0, has_side_effects=True, vmem_limit_bytes=56 * 1024 * 1024
        ),
    )(hidden, conv_weight, feat_query_w, feat_key_w, win_query, win_key, selq, rowq)


def solution(mesh):
    placed = (P(("groups", "seq"), None), P(), P(), P(), P(("groups", "seq"), None), P(("groups", "seq"), None))
    return jax.shard_map(
        functools.partial(local, mesh.shape["seq"]),
        mesh=mesh, in_specs=placed, out_specs=P(("groups", "seq"), None), check_vma=False,
    )
```

```python
import functools

import jax
import jax.numpy as jnp
import numpy as np
from jax import lax
from jax.experimental import pallas as pl
from jax.experimental.pallas import tpu as pltpu
from jax.sharding import PartitionSpec as P

HEADS = 16
FEAT = 16
WINDOW = 64
CHIPS = 4
CORES = 2
TEAM = CHIPS * CORES
HALF = HEADS // CORES
OWN = HALF // CHIPS
CUTS = 1
PIECES = OWN * CUTS
ROWS = 160
QUADS = 136
GROUP = 4
TURNV = 1
LAGB = 1
PAIR = 2
TURN0 = 2
PER0 = 1
TURN1 = 6
PER1 = 1
TURNT = 3
BF = jnp.bfloat16
F32 = jnp.float32


def tables(block):
    half = FEAT // 2
    tiles = [[(i, (i + d) % half) for i in range(half)] for d in range(4)]
    tiles += [[(half + i, half + (i + d) % half) for i in range(half)] for d in range(4)]
    tiles += [[(i, half + (i + d) % half) for i in range(half)] for d in range(half)]
    tiles += [[(i, i + 4) if i < 4 else (half + i, half + i - 4) for i in range(half)]]
    sel_q = np.zeros((FEAT, 512), np.float32)
    rows_q = np.zeros((8, 256), np.float32)
    for f, (i, j) in enumerate(sum(tiles, [])):
        sel_q[i, f] = 1.0
        sel_q[j, 256 + f] = 0.5 / FEAT * (1.0 if i == j else 2.0)
    for i in range(FEAT):
        sel_q[i, QUADS + i] = 1.0
        rows_q[1, QUADS + i] = FEAT**-0.5
    rows_q[0, QUADS + FEAT] = 1.0
    rows_q[1, QUADS + FEAT] = 1.0
    return jnp.asarray(np.tile(sel_q, (block // FEAT, 1)), BF), jnp.asarray(rows_q, F32)


def nt(a, b):
    return lax.dot_general(a, b, (((1,), (1,)), ((), ())), preferred_element_type=F32)


def nn(a, b):
    return jnp.dot(a, b, preferred_element_type=F32)


def kernel(
    n, hid_h, cw_h, wq_h, wk_h, qry_h, key_h, selq_h, rowq_h, out,
    hid, cw, wq, wk, qry, key, selq, rowq,
    hprev, kprev, vprev, cv, fqs, fks, fkt, fkf, st, rbuf, xs, rin, cin, cout, ag, bin_, obuf, sbuf, phs,
    ywin, num, den, wbias, cmask,
    loads, hs_send, hs_recv, v_send, v_recv, a_send, a_recv, r_send, r_recv, c_send, c_recv, g_send, g_recv, b_send, b_recv,
):
    count, width = hid.shape
    head = width // HEADS
    me = lax.axis_index("seq")
    team = me // TEAM
    core = lax.rem(me, CORES)
    chip = lax.rem(me // CORES, CHIPS)
    teams = n // TEAM
    has_prev, has_next = me > 0, me < n - 1
    has_up, has_down = team > 0, team < teams - 1
    sibling = me + 1 - 2 * core
    mine_at, theirs_at = core * HALF, (1 - core) * HALF

    def member(other):
        return team * TEAM + other * CORES + core

    barrier = pltpu.get_barrier_semaphore()

    def hello(dev):
        pl.semaphore_signal(barrier, inc=1, device_id={"seq": dev}, device_id_type=pl.DeviceIdType.MESH)

    hello(sibling)
    for d in range(1, CHIPS):
        hello(member(lax.rem(chip + d, CHIPS)))
    pl.when(has_prev)(lambda: hello(me - 1))
    pl.when(has_next)(lambda: hello(me + 1))
    pl.when(has_up)(lambda: hello(me - TEAM))
    pl.when(has_down)(lambda: hello(me + TEAM))
    pairs = ((hid_h, hid), (cw_h, cw), (selq_h, selq), (rowq_h, rowq))
    fetch = [pltpu.make_async_copy(a, b, loads.at[i]) for i, (a, b) in enumerate(pairs)]

    def by_columns(a, b, sem):
        for h in range(a.shape[1] // head):
            pltpu.make_async_copy(a.at[:, pl.ds(h * head, head)], b.at[h], sem).start()

    fetch[0].start()
    fetch[1].start()
    by_columns(wk_h, wk, loads.at[4])
    by_columns(key_h, key, loads.at[6])
    by_columns(wq_h, wq, loads.at[5])
    by_columns(qry_h, qry, loads.at[7])
    fetch[2].start()
    fetch[3].start()
    fetch += [pltpu.make_async_copy(a, a, loads.at[4 + i]) for i, a in enumerate((wk, wq, key, qry))]

    greeted = CHIPS
    for there in (has_prev, has_next, has_up, has_down):
        greeted = greeted + there.astype(jnp.int32)
    pl.semaphore_wait(barrier, greeted)

    def remote(src, dst, send, recv, dev):
        return pltpu.make_async_remote_copy(
            src_ref=src, dst_ref=dst, send_sem=send, recv_sem=recv,
            device_id={"seq": dev}, device_id_type=pl.DeviceIdType.MESH,
        )

    tail_copy = remote(hid_h.at[pl.ds(count - 16, 16)], hprev, hs_send.at[0], hs_recv.at[0], me + 1)
    key_copy = remote(key.at[:, pl.ds(count - WINDOW, WINDOW)], kprev, hs_send.at[1], hs_recv.at[1], me + 1)

    def val_copy(g):
        part = pl.ds(g * GROUP, GROUP)
        return remote(cv.at[part, pl.ds(count - WINDOW, WINDOW)], vprev.at[part], v_send.at[g], v_recv.at[g], me + 1)


    pl.when(has_next)(lambda: tail_copy.start())
    fetch[6].wait()
    pl.when(has_next)(lambda: key_copy.start())

    @pl.when(jnp.logical_not(has_prev))
    def _():
        hprev[...] = jnp.zeros_like(hprev)
        kprev[...] = jnp.zeros_like(kprev)
        vprev[...] = jnp.zeros_like(vprev)

    r = lax.broadcasted_iota(jnp.int32, (count, head), 0)
    j = lax.broadcasted_iota(jnp.int32, (count, head), 1)
    rr = lax.rem(r, WINDOW)
    first = jnp.where(has_prev, 0, WINDOW)
    j = jnp.where(lax.rem(r // WINDOW, 2) == 1, lax.rem(j + WINDOW, 2 * WINDOW), j)
    ok = (j > rr) & (j <= rr + WINDOW) & ((j >= first) | (r >= WINDOW))
    wbias[...] = jnp.where(ok, 0.0, -1e30)
    half = count // 2
    r = lax.broadcasted_iota(jnp.int32, (half, half), 0)
    j = lax.broadcasted_iota(jnp.int32, (half, half), 1)
    cmask[...] = jnp.where(j <= r, 1.0, 0.0)

    fetch[0].wait()
    fetch[1].wait()
    wide = 2 * head
    edge = 16

    def conv_step(b, c):
        cols = pl.ds(pl.multiple_of(b * wide, wide), wide)
        h = hid[:, cols].astype(F32)
        w = cw[:, cols]
        v = (w[0:1] * pltpu.roll(h, 2, 0) + w[1:2] * pltpu.roll(h, 1, 0) + w[2:3] * h).astype(BF)
        cv[2 * b] = v[:, :head]
        cv[2 * b + 1] = v[:, head:]
        return c

    lax.fori_loop(0, width // wide, conv_step, 0)
    fetch[4].wait()
    fetch[5].wait()

    def project(rows):
        f = nn(
            jnp.concatenate([cv[h, rows] for h in range(HEADS)], axis=1),
            jnp.concatenate([wk[0], wk[1], wq[0], wq[1]], axis=1),
        ).astype(BF)
        fks[rows] = f[:, :256].astype(F32)
        for b in range(2):
            fqs[b, rows] = f[:, 256 + b * 128 : 256 + (b + 1) * 128]

    project(slice(edge, count))

    pl.when(has_prev)(lambda: tail_copy.wait_recv())
    row = lax.broadcasted_iota(jnp.int32, (edge, wide), 0)
    for b in range(width // wide):
        cols = slice(b * wide, (b + 1) * wide)
        h = hid[:edge, cols].astype(F32)
        hp = hprev[:, cols].astype(F32)
        h1 = jnp.where(row == 0, hp[15:16], pltpu.roll(h, 1, 0))
        h2 = jnp.where(row == 0, hp[14:15], jnp.where(row == 1, hp[15:16], pltpu.roll(h, 2, 0)))
        w = cw[:, cols]
        v = (w[0:1] * h2 + w[1:2] * h1 + w[2:3] * h).astype(BF)
        cv[2 * b, :edge] = v[:, :head]
        cv[2 * b + 1, :edge] = v[:, head:]
    project(slice(0, edge))
    fk = fks[...]
    fk = fk.T
    fkf[...] = fk
    fkt[...] = fk.astype(BF)

    small = FEAT // 2
    srow = lax.broadcasted_iota(jnp.int32, (small, count), 0)
    unit = jnp.where(srow == 0, 1.0, 0.0)
    er = lax.broadcasted_iota(jnp.int32, (head, head), 0)
    ec = lax.broadcasted_iota(jnp.int32, (head, head), 1)
    eye = er == ec
    trow = lax.broadcasted_iota(jnp.int32, (16, head), 0)
    ones_v = jnp.ones((count, head), BF)

    def turned8(x, d):
        return pltpu.roll(x, small - d, 0) if d else x

    def key_features(h):
        k = fkf[pl.ds(pl.multiple_of(h * FEAT, FEAT), FEAT), :]
        lo, hi = k[:small], k[small:]
        rl = [turned8(lo, d) for d in range(5)]
        rh = [turned8(hi, d) for d in range(small)]
        tiles = [lo * rl[d] for d in range(4)] + [hi * rh[d] for d in range(4)]
        tiles += [lo * rh[d] for d in range(small)]
        tiles += [jnp.where(srow < 4, lo, hi) * jnp.where(srow < 4, rl[4], rh[4])]
        return jnp.concatenate(tiles + [lo, hi, unit], axis=0).astype(BF)

    def make_states(hs):
        ps = [key_features(h) for h in hs]
        vs = [cv[h] for h in hs]
        ss = [nn(p, jnp.concatenate([v, ones_v], axis=1)) for p, v in zip(ps, vs)]
        res = []
        for s in ss:
            col = s[:, head:]
            row_a = jnp.sum(jnp.where(eye, col[:head], 0.0), axis=0, keepdims=True)
            row_b = jnp.sum(jnp.where(eye[: ROWS - head], col[head:], 0.0), axis=0, keepdims=True)
            tail = jnp.where(trow == 9, row_a, jnp.where(trow == 10, row_b, s[144:, :head]))
            res.append(jnp.concatenate([s[:144, :head], tail], axis=0).astype(BF))
        for h, r in zip(hs, res):
            st[h] = r

    def to_sibling(p):
        return remote(st.at[theirs_at + p], rbuf.at[p], a_send.at[0], a_recv.at[p], sibling)

    def rows(b):
        return pl.ds(pl.multiple_of(b * (ROWS // CUTS), 16), ROWS // CUTS)

    def scatter(p, b):
        at = chip * PIECES + lax.rem(p, OWN) * CUTS + b
        return remote(
            xs.at[p, rows(b)], rin.at[chip, lax.rem(p, OWN), rows(b)], r_send.at[0], r_recv.at[at], member(p // OWN)
        )

    def scattered(other, j, b):
        return remote(xs.at[0, rows(b)], rin.at[other, j, rows(b)], r_send.at[0], r_recv.at[other * PIECES + j * CUTS + b], me)

    def chain(j, b):
        q = j * CUTS + b
        return remote(cout.at[j, rows(b)], cin.at[j, rows(b)], c_send.at[0], c_recv.at[q], me + TEAM)

    def gather(other, j, b):
        q = j * CUTS + b
        return remote(
            ag.at[other, j, rows(b)], bin_.at[chip * OWN + j, rows(b)],
            g_send.at[0], g_recv.at[chip * PIECES + q], member(other),
        )

    def gathered(p, b):
        return remote(ag.at[0, 0, rows(b)], bin_.at[p, rows(b)], g_send.at[0], g_recv.at[p * CUTS + b], me)

    def back(p):
        return remote(obuf.at[p], sbuf.at[mine_at + p], b_send.at[0], b_recv.at[p], sibling)

    def nth(s):
        return lax.rem(chip + 1 + lax.rem(s, CHIPS), CHIPS) * OWN + s // CHIPS

    def needed(p):
        return has_down | (chip < CHIPS - 1)

    def pass_on(p):
        to_sibling(p).wait_recv()
        both = (st[mine_at + p].astype(F32) + rbuf[p].astype(F32)).astype(BF)
        away = p // OWN != chip

        @pl.when(away & needed(p))
        def _():
            xs[p] = both
            for b in range(CUTS):
                scatter(p, b).start()

        @pl.when(jnp.logical_not(away))
        def _():
            rin[chip, lax.rem(p, OWN)] = both

    def pair(t):
        return [nth(2 * t), nth(2 * t + 1)]

    def send(ps):
        for p in ps:
            to_sibling(p).start()

    def states(t, carry):
        now, later = pair(t), pair(t + 1)
        make_states([theirs_at + p for p in later] + [mine_at + p for p in now])
        send(later)
        for p in now:
            pass_on(p)
        return carry

    make_states([theirs_at + p for p in pair(0)])
    send(pair(0))
    lax.fori_loop(0, HALF // 2 - 1, states, 0)
    make_states([mine_at + p for p in pair(HALF // 2 - 1)])
    for p in pair(HALF // 2 - 1):
        pass_on(p)

    def send_values(i):
        @pl.when(has_next & (i == TURNV))
        def _():
            for g in range(HEADS // GROUP):
                val_copy(g).start()

    def own(q):
        j, b = q // CUTS, lax.rem(q, CUTS)
        part = rows(b)
        for d in range(1, CHIPS):
            other = lax.rem(chip + d, CHIPS)
            pl.when(has_down | (other < CHIPS - 1))(lambda: scattered(other, j, b).wait_recv())

        @pl.when(has_up)
        def _():
            chain(j, b).wait_recv()

        @pl.when(jnp.logical_not(has_up))
        def _():
            cin[j, part] = jnp.zeros_like(cin[j, part])

        before = cin[j, part].astype(F32)

        @pl.when(has_down)
        def _():
            total = before
            for k in range(CHIPS):
                total = total + rin[k, j, part].astype(F32)
            cout[j, part] = total.astype(BF)
            chain(j, b).start()

        for k in range(CHIPS):
            ag[k, j, part] = before.astype(BF)
            pl.when(chip != k)(lambda k=k: gather(k, j, b).start())
            if k < CHIPS - 1:
                before = before + rin[k, j, part].astype(F32)
        bin_[chip * OWN + j, part] = ag[chip, j, part]

    last = 2 * HEADS // GROUP
    turn0 = jnp.where(has_up, TURN1 + TURNT * (team - 1), TURN0)
    per = jnp.where(has_up, PER1, PER0)

    def events(i):
        def one(q, carry):
            own(q)
            return carry

        first = jnp.clip((i - turn0) * per, 0, PIECES)
        lax.fori_loop(first, jnp.clip((i + 1 - turn0) * per, 0, PIECES), one, 0)

    lane = lax.broadcasted_iota(jnp.int32, (8, 128), 1)

    def masked_query(h):
        mask = jnp.where(lane // FEAT == lax.rem(h, 8), 1.0, 0.0)[0:1].astype(BF)
        return fqs[h // 8] * mask

    lin, sq = FEAT**-0.5, 0.5 / FEAT

    def columns(h):
        return pl.ds(pl.multiple_of(h * head, head), head)

    def linear_steps(hs):
        ms = [masked_query(h) for h in hs]
        kt = fkt[pl.ds(pl.multiple_of((hs[0] // 8) * 128, 128), 128), :]
        vbs = [jnp.concatenate([cv[h], ones_v], axis=1) for h in hs]
        x = nn(jnp.concatenate([m[:half] for m in ms], axis=0), kt[:, :half])
        a = 1.0 + x * (lin + sq * x)
        top = [(a[i * half : (i + 1) * half] * cmask[...]).astype(BF) for i in range(len(hs))]
        x = nn(jnp.concatenate([m[half:] for m in ms], axis=0), kt)
        a = 1.0 + x * (lin + sq * x)
        low = [a[i * half : (i + 1) * half] for i in range(len(hs))]
        low = [jnp.concatenate([b[:, :half], b[:, half:] * cmask[...]], axis=1).astype(BF) for b in low]
        tops = [nn(a, vb[:half]) for a, vb in zip(top, vbs)]
        lows = [nn(a, vb) for a, vb in zip(low, vbs)]
        for h, a, b in zip(hs, tops, lows):
            num[:half, columns(h)] = a[:, :head]
            den[:half, columns(h)] = a[:, head:]
            num[half:, columns(h)] = b[:, :head]
            den[half:, columns(h)] = b[:, head:]

    left = lax.broadcasted_iota(jnp.int32, (WINDOW, head), 1) < WINDOW
    ones_w = jnp.ones((2 * WINDOW, head), BF)
    scale = head**-0.5 * np.log2(np.e)

    def scores(h):
        q = qry[h]
        k = jnp.concatenate([kprev[h], key[h]], axis=0)
        w = WINDOW
        a = nt(q[: 2 * w], k[: 2 * w])
        b = nt(q[w : 3 * w], k[2 * w : 4 * w])
        c = nt(q[3 * w :], jnp.concatenate([k[4 * w :], k[3 * w : 4 * w]], axis=0))
        s = jnp.concatenate([a[:w], jnp.where(left, b[:w], a[w:]), b[w:], c], axis=0)
        return s * scale + wbias[...]

    def blend(h, p):
        w = WINDOW
        v = [vprev[h]] + [cv[h, i * w : (i + 1) * w] for i in range(count // w)]
        ys = []
        for i in range(count // w):
            pair = v[i : i + 2] if i % 2 == 0 else [v[i + 1], v[i]]
            ys.append(nn(p[i * w : (i + 1) * w], jnp.concatenate([jnp.concatenate(pair, axis=0), ones_w], axis=1)))
        return jnp.concatenate(ys, axis=0)

    def window_steps(hs):
        ss = [scores(h) for h in hs]
        ps = [jnp.exp2(s - jnp.max(s, axis=-1, keepdims=True)).astype(BF) for s in ss]
        ys = [blend(h, p) for h, p in zip(hs, ps)]
        ys = [y[:, :head] / y[:, head:] for y in ys]
        for h, y in zip(hs, ys):
            ywin[:, columns(h)] = y

    def feature_steps(hs):
        lr = nn(jnp.concatenate([masked_query(h) for h in hs], axis=0), selq[...])
        f = ((lr[:, :256] + rowq[0:1]) * (lr[:, 256:] + rowq[1:2])).astype(BF)
        for i, h in enumerate(hs):
            phs[h] = f[i * count : (i + 1) * count]

    steps = HEADS // GROUP

    for copy in (fetch[2], fetch[3], fetch[7]):
        copy.wait()

    def linear(i, carry):
        send_values(i)
        events(i)
        hs = [GROUP * i + d for d in range(GROUP)]
        feature_steps(hs)
        linear_steps(hs)
        return carry

    lax.fori_loop(0, steps, linear, 0)

    pl.when(has_prev)(lambda: key_copy.wait_recv())

    def window(i, carry):
        events(steps + i)
        pl.when(has_prev)(lambda: val_copy(i).wait_recv())
        window_steps([GROUP * i + d for d in range(GROUP)])
        return carry

    lax.fori_loop(0, steps, window, 0)

    def late(q, carry):
        own(q)
        return carry

    lax.fori_loop(jnp.clip((last - turn0) * per, 0, PIECES), PIECES, late, 0)

    own_first = jnp.where(core == 0, 1.0, 0.0)
    spare = jnp.zeros((256 - ROWS, 2 * head), BF)

    ones_h = jnp.ones((head, head), BF)

    def final_steps(hs):
        ws = []
        for h in hs:
            s = sbuf[h]
            t = s[144:].astype(F32)
            d = jnp.concatenate(
                [jnp.where(eye, t[9:10], 0.0), jnp.where(eye[: ROWS - head], t[10:11], 0.0)], axis=0
            ).astype(BF)
            ws.append((s, d))
        ws = [(s, nn(d, ones_h).astype(BF)) for s, d in ws]
        ws = [jnp.concatenate([jnp.concatenate([s, c], axis=1), spare], axis=0) for s, c in ws]
        rs = [nn(phs[h], w) for h, w in zip(hs, ws)]
        ys = []
        for h, r in zip(hs, rs):
            cols = pl.ds(pl.multiple_of(h * head, head), head)
            ys.append((ywin[:, cols] + (num[:, cols] + r[:, :head]) / (den[:, cols] + r[:, head:])).astype(BF))
        for h, y in zip(hs, ys):
            out[:, pl.ds(pl.multiple_of(h * head, head), head)] = y

    def turned(u):
        late = u - OWN
        other = lax.rem(chip + 1 + lax.rem(late, CHIPS - 1), CHIPS)
        return jnp.where(u < OWN, chip * OWN + u, other * OWN + late // (CHIPS - 1))

    def give_back(p):
        @pl.when(p // OWN != chip)
        def _():
            for b in range(CUTS):
                gathered(p, b).wait_recv()

        before = bin_[p].astype(F32)
        at = mine_at + p
        obuf[p] = (before + own_first * st[at].astype(F32)).astype(BF)
        back(p).start()
        sbuf[at] = (before + (1.0 - own_first) * rbuf[p].astype(F32)).astype(BF)

    @pl.when(has_next)
    def _():
        tail_copy.wait_send()
        key_copy.wait_send()
        for g in range(HEADS // GROUP):
            val_copy(g).wait_send()

    remote(st.at[pl.ds(0, HALF)], st.at[pl.ds(0, HALF)], a_send.at[0], a_recv.at[0], sibling).wait_send()

    @pl.when(has_down | (chip < CHIPS - 1))
    def _():
        away = pl.ds(0, HALF - OWN)
        remote(xs.at[away], xs.at[away], r_send.at[0], r_recv.at[0], sibling).wait_send()

    def wind_up(u, carry):
        @pl.when(u < HALF // PAIR)
        def _():
            for i in range(PAIR):
                give_back(turned(PAIR * u + i))

        @pl.when(u >= LAGB)
        def _():
            ps = [turned(PAIR * (u - LAGB) + i) for i in range(PAIR)]
            for p in ps:
                back(p).wait_recv()
            final_steps([at + p for p in ps for at in (mine_at, theirs_at)])

        return carry

    lax.fori_loop(0, HALF // PAIR + LAGB, wind_up, 0)

    remote(obuf, obuf, b_send.at[0], b_recv.at[0], sibling).wait_send()
    away = pl.ds(0, CHIPS - 1)
    remote(ag.at[away], ag.at[away], g_send.at[0], g_recv.at[0], sibling).wait_send()
    pl.when(has_down)(lambda: remote(cout, cout, c_send.at[0], c_recv.at[0], sibling).wait_send())


def local(n, hidden, conv_weight, feat_query_w, feat_key_w, win_query, win_key):
    count, width = hidden.shape
    head = width // HEADS
    selq, rowq = tables(128)
    half = (HALF, ROWS, head)
    dma = pltpu.SemaphoreType.DMA
    return pl.pallas_call(
        functools.partial(kernel, n),
        out_shape=pltpu.VMEM((count, width), BF),
        in_specs=[pl.BlockSpec(memory_space=pl.ANY)] * 8,
        out_specs=pl.BlockSpec(memory_space=pltpu.VMEM),
        scratch_shapes=[
            pltpu.VMEM((count, width), BF),
            pltpu.VMEM(conv_weight.shape, F32),
            pltpu.VMEM((2, width, head), BF),
            pltpu.VMEM((2, width, head), BF),
            pltpu.VMEM((HEADS, count, head), BF),
            pltpu.VMEM((HEADS, count, head), BF),
            pltpu.VMEM(selq.shape, BF),
            pltpu.VMEM(rowq.shape, F32),
            pltpu.VMEM((16, width), BF),
            pltpu.VMEM((HEADS, WINDOW, head), BF),
            pltpu.VMEM((HEADS, WINDOW, head), BF),
            pltpu.VMEM((HEADS, count, head), BF),
            pltpu.VMEM((2, count, 128), BF),
            pltpu.VMEM((count, 256), F32),
            pltpu.VMEM((256, count), BF),
            pltpu.VMEM((256, count), F32),
            pltpu.VMEM((HEADS, ROWS, head), BF),
            pltpu.VMEM(half, BF),
            pltpu.VMEM(half, BF),
            pltpu.VMEM((CHIPS, OWN, ROWS, head), BF),
            pltpu.VMEM((OWN, ROWS, head), BF),
            pltpu.VMEM((OWN, ROWS, head), BF),
            pltpu.VMEM((CHIPS, OWN, ROWS, head), BF),
            pltpu.VMEM(half, BF),
            pltpu.VMEM(half, BF),
            pltpu.VMEM((HEADS, ROWS, head), BF),
            pltpu.VMEM((HEADS, count, 256), BF),
            pltpu.VMEM((count, width), F32),
            pltpu.VMEM((count, width), F32),
            pltpu.VMEM((count, width), F32),
            pltpu.VMEM((count, head), F32),
            pltpu.VMEM((count // 2, count // 2), F32),
            dma((8,)), dma((2,)), dma((2,)),
            dma((HEADS // GROUP,)), dma((HEADS // GROUP,)),
        ]
        + [
            dma((1,)), dma((HALF,)), dma((1,)), dma((HALF * CUTS,)), dma((1,)), dma((PIECES,)),
            dma((1,)), dma((HALF * CUTS,)), dma((1,)), dma((HALF,)),
        ],
        compiler_params=pltpu.CompilerParams(
            collective_id=0, has_side_effects=True, vmem_limit_bytes=56 * 1024 * 1024
        ),
    )(hidden, conv_weight, feat_query_w, feat_key_w, win_query, win_key, selq, rowq)


def solution(mesh):
    placed = (P(("groups", "seq"), None), P(), P(), P(), P(("groups", "seq"), None), P(("groups", "seq"), None))
    return jax.shard_map(
        functools.partial(local, mesh.shape["seq"]),
        mesh=mesh, in_specs=placed, out_specs=P(("groups", "seq"), None), check_vma=False,
    )
```
